32 devices in a mesh: leaf: 4 (over y, core), panel: 8 (over z, x).
Axes of the slice: x: 2, y: 2, z: 4, core: 2. Of those that a mesh axis runs over, the one named last changes fastest.
Arguments:
- root_entries: float32 [2048, 2048], P('leaf', 'panel'), as said below
- child_updates: bfloat16 [2048, 1024], P('leaf', 'panel'), as said below
- child_map: int32 [2, 1024], replicated, may hold values from 0 to 2047, as said below
- tile_pattern: int32 [2, 8, 8], replicated, may hold values 0 or 1
Outputs:
- factored: float32 [2048, 2048], P('leaf', 'panel')
The draws below stay inside these ranges and needn't reach their ends.
Inputs may be any that keep to these rules, and one draw needn't show every extreme that they name: `root_entries`: symmetric and positive definite. `child_updates`: each child's block of 1024 rows is symmetric. `child_map`: each row holds 1024 distinct rows of the root front.
All inputs are finite; a program needn't handle non-finite values.
Results may differ from the reference program's by a relative error of at most 0.0003.
Values may be sent and summed in bfloat16 or wider, within the bound.
No kernel may reach another device: no remote copies, remote signals or barrier semaphores. Data moves between devices by JAX's collectives and lax.ppermute only.
A program may use at most 64 MiB of HBM per device.

```python
import math
import jax
import jax.numpy as jnp
from jax import lax

PANEL = 256
TILE = 128
STEPS = 5
FRONT = 2048
CHILD = 1024


def draw_root_entries(key, part):
    place_key, space_key, scale_key, noise_key, shift_key = jax.random.split(key, 5)
    jitter = jax.random.uniform(place_key, (FRONT,), jnp.float32, -0.5, 0.5)
    moments = (jnp.arange(FRONT).astype(jnp.float32) + jitter) / PANEL
    places = jax.random.uniform(space_key, (FRONT,), jnp.float32)
    distance = 4.0 * jnp.abs(moments[:, None] - moments[None, :]) + 2.0 * jnp.abs(places[:, None] - places[None, :])
    kernel = jnp.exp(-distance)
    spread = math.sqrt(FRONT)
    scales = jax.random.uniform(scale_key, (FRONT,), jnp.float32, 1.0, 1.8)
    sampled = jax.random.truncated_normal(noise_key, -6.0, 6.0, (FRONT, FRONT), jnp.float32)
    lifted = jax.random.uniform(shift_key, (FRONT,), jnp.float32, 0.18 * spread, 0.36 * spread)
    coupling = scales[:, None] * scales[None, :] * kernel
    roughness = (sampled + sampled.T) * (0.02 / math.sqrt(2.0))
    identity = jnp.arange(FRONT)[:, None] == jnp.arange(FRONT)[None, :]
    return jnp.where(identity, coupling + lifted[:, None], coupling + roughness).astype(jnp.float32)


def draw_child_updates(key, part):
    sampled = jax.random.truncated_normal(key, -6.0, 6.0, (2, CHILD, CHILD), jnp.float32)
    mirrored = (sampled + jnp.swapaxes(sampled, 1, 2)) * (0.05 / math.sqrt(2.0))
    return mirrored.reshape(2 * CHILD, CHILD).astype(jnp.bfloat16)


def draw_child_map(key, part):
    rows = []
    for which in range(2):
        order = jax.random.permutation(jax.random.fold_in(key, which + 11), FRONT)
        rows.append(order[:CHILD])
    return jnp.stack(rows).astype(jnp.int32)


def place_ends(array, own_key, least, largest):
    longest = array.shape.index(max(array.shape))
    spots = []
    for shift in (0, 1):
        where = [jax.random.randint(jax.random.fold_in(own_key, axis), (), 0, length) for axis, length in enumerate(array.shape)]
        where[longest] = (where[longest] + shift) % array.shape[longest]
        spots.append(tuple(where))
    return array.at[spots[0]].set(least).at[spots[1]].set(largest)


def setup_inputs(seed: int = 0) -> dict:
    keys = jax.random.split(jax.random.key(seed), 5)
    root_entries = draw_root_entries(jax.random.fold_in(keys[4], 71), 0)
    child_updates = draw_child_updates(jax.random.fold_in(keys[4], 71), 0)
    child_map = draw_child_map(jax.random.fold_in(keys[4], 71), 0)
    tile_pattern = place_ends((jax.random.randint(keys[3], (2, CHILD // TILE, CHILD // TILE), 0, 3) < 2).astype(jnp.int32), jax.random.fold_in(keys[3], 1), 0, 1)
    return {"root_entries": root_entries, "child_updates": child_updates, "child_map": child_map, "tile_pattern": tile_pattern}


def reference(root_entries, child_updates, child_map, tile_pattern):
    extended = jnp.zeros((FRONT, FRONT), jnp.float32)
    for which in range(2):
        pattern = tile_pattern[which]
        mirrored = jnp.maximum(pattern, pattern.T)
        spread = jnp.repeat(jnp.repeat(mirrored, TILE, axis=0), TILE, axis=1)
        block = child_updates[which * CHILD:(which + 1) * CHILD].astype(jnp.float32)
        kept = jnp.where(spread > 0, block, jnp.float32(0.0))
        targets = child_map[which].astype(jnp.int32)
        extended = extended.at[targets[:, None], targets[None, :]].add(kept)
    front = root_entries + extended
    for step in range(STEPS):
        first = step * PANEL
        last = first + PANEL
        pivot_factor = jnp.linalg.cholesky(front[first:last, first:last])
        below = lax.linalg.triangular_solve(pivot_factor, front[last:, first:last], left_side=False, lower=True, transpose_a=True)
        column = jnp.concatenate([jnp.zeros((first, PANEL), jnp.float32), pivot_factor, below], axis=0)
        front = front.at[:, first:last].set(column)
        front = front.at[last:, last:].add(-jnp.dot(below, below.T, precision=lax.Precision.HIGHEST))
    done = STEPS * PANEL
    front = front.at[:done, done:].set(jnp.float32(0.0))
    return front
```

```python
import functools

import jax
import jax.numpy as jnp
from jax import lax
from jax.experimental import pallas as pl
from jax.experimental.pallas import tpu as pltpu
from jax.sharding import PartitionSpec as P

PANEL = 256
STEPS = 5
HALF = PANEL // 2
SUB = 8
DONE = STEPS * PANEL
HIGHEST = lax.Precision.HIGHEST
F32 = jnp.float32
BF16 = jnp.bfloat16
SMEM_SPEC = pl.BlockSpec(memory_space=pltpu.SMEM)
VMEM_SPEC = pl.BlockSpec(memory_space=pltpu.VMEM)


def mm(a, b, precision=None):
    return lax.dot_general(
        a, b, (((1,), (0,)), ((), ())), precision=precision, preferred_element_type=F32
    )


def mm_nt(a, b, precision=None):
    return lax.dot_general(
        a, b, (((1,), (1,)), ((), ())), precision=precision, preferred_element_type=F32
    )


def factor_half(a):
    n = a.shape[0]
    groups = n // SUB
    rows = [a[SUB * g : SUB * g + SUB, :] for g in range(groups)]
    lane = lax.broadcasted_iota(jnp.int32, (SUB, n), 1)
    sub = lax.broadcasted_iota(jnp.int32, (SUB, n), 0)
    inv = [jnp.where(lane == sub + SUB * g, 1.0, 0.0).astype(F32) for g in range(groups)]

    def full(v):
        return jnp.broadcast_to(v, (SUB, n))

    for g in range(groups):
        left = groups - g
        col = [
            [full(rows[g + h][:, SUB * g + q : SUB * g + q + 1]) for h in range(left)]
            for q in range(SUB)
        ]
        tip = [[full(col[q][0][r : r + 1, :]) for r in range(SUB)] for q in range(SUB)]
        scale = jnp.zeros((SUB, n), F32)
        for q in range(SUB):
            pivot = tip[q][q]
            recip = 1.0 / pivot
            scale = jnp.where(sub == q, lax.rsqrt(pivot), scale)
            part = [tip[q][r] * recip for r in range(SUB)]
            for q2 in range(q + 1, SUB):
                for r in range(q2, SUB):
                    tip[q2][r] = tip[q2][r] - part[r] * tip[q][q2]
            mult = [col[q][h] * recip for h in range(left)]
            mult[0] = jnp.where(sub > q, mult[0], 0.0)
            for q2 in range(q + 1, SUB):
                for h in range(left):
                    col[q2][h] = col[q2][h] - mult[h] * tip[q][q2]
            row_a = full(rows[g][q : q + 1, :])
            row_w = full(inv[g][q : q + 1, :])
            for h in range(left):
                rows[g + h] = rows[g + h] - mult[h] * row_a
                inv[g + h] = inv[g + h] - mult[h] * row_w
        rows[g] = rows[g] * scale
        inv[g] = inv[g] * scale
    upper = jnp.concatenate(rows, 0)
    r = lax.broadcasted_iota(jnp.int32, (n, n), 0)
    c = lax.broadcasted_iota(jnp.int32, (n, n), 1)
    return jnp.where(r <= c, upper, 0.0), jnp.concatenate(inv, 0)


def select_kernel(bases_ref, keep_ref, map_ref, *refs):
    pieces, out_ref = refs[:-1], refs[-1]
    width = pieces[0].shape[1]
    tiles = keep_ref.shape[0]
    tile = pieces[0].shape[0] // tiles
    block = pl.program_id(0)
    ids = lax.broadcasted_iota(jnp.int32, (PANEL, 1), 0) + bases_ref[block]
    total = jnp.zeros(out_ref.shape[1:], F32)
    for k, piece in enumerate(pieces):
        kept = jnp.concatenate(
            [
                piece[t * tile : (t + 1) * tile, :] * keep_ref[t, k].astype(F32).astype(BF16)
                for t in range(tiles)
            ],
            0,
        )
        hot = (ids == map_ref[:, k * width : (k + 1) * width]).astype(F32).astype(BF16)
        total = total + mm_nt(kept, hot)
    out_ref[0] = total.astype(BF16)


def placed(row_base, count, map_ref, pieces):
    width = pieces[0].shape[0]
    ids = lax.broadcasted_iota(jnp.int32, (count, 1), 0) + row_base
    total = None
    for x, piece in enumerate(pieces):
        hot = (ids == map_ref[:, x * width : (x + 1) * width]).astype(F32).astype(BF16)
        term = mm(hot, piece[...])
        total = term if total is None else total + term
    return total


def step_kernel(step, leaves, spots, *refs):
    place_ref, map_ref = refs[0], refs[1]
    refs = refs[2:]
    own_col, refs = refs[:leaves], refs[leaves:]
    step_col, refs = refs[:leaves], refs[leaves:]
    root_own, refs = refs[:spots], refs[spots:]
    root_step, refs = refs[:spots], refs[spots:]
    root_mine, refs = refs[0], refs[1:]
    before_a, refs = refs[:step], refs[step:]
    before_r, refs = refs[:step], refs[step:]
    before_y, refs = refs[:step], refs[step:]
    later = STEPS - 1 - step
    if later:
        xa_ref, refs = refs[0], refs[1:]
    xr_ref, y_ref, l_ref, li_ref, root_s, rown_s, d_s, t_s = refs
    device_rows = xr_ref.shape[0]
    per_leaf = device_rows // PANEL
    for x in range(spots):
        leaf = place_ref[2 + x]
        root_s[leaf] = root_step[x][...]
        rown_s[leaf] = root_own[x][...]

    def root_rows(scratch, r):
        return scratch[r // per_leaf, pl.ds(r % per_leaf * PANEL, PANEL), :].astype(F32)

    def mine(m):
        return before_a[m][(step - m - 1) * PANEL : (step - m) * PANEL, :]

    first = step * PANEL
    diag = root_rows(root_s, step) + root_s[step // per_leaf, pl.ds(device_rows, PANEL), :].astype(F32)
    diag = diag + placed(first, PANEL, map_ref, step_col)
    for m in range(step):
        diag = diag - mm_nt(mine(m), mine(m))
    d_s[0] = diag[:HALF, :HALF]
    d_s[1] = diag[HALF:, HALF:]
    l21 = diag[HALF:, :HALF]
    l_ref[HALF:, :HALF] = l21

    def half(h, carry):
        t, i = factor_half(d_s[h])
        t_s[2 * h] = t
        t_s[2 * h + 1] = i

        @pl.when(h == 0)
        def _():
            low = mm_nt(l_ref[HALF:, :HALF], i, HIGHEST)
            l_ref[HALF:, :HALF] = low
            d_s[1] = d_s[1] - mm_nt(low, low, HIGHEST)

        return carry

    lax.fori_loop(0, 2, half, 0)
    i1, i2 = t_s[1], t_s[3]
    i21 = -mm(i2, mm(l_ref[HALF:, :HALF], i1, HIGHEST), HIGHEST)
    empty = jnp.zeros((HALF, HALF), F32)
    li_ref[:HALF, :HALF] = i1
    li_ref[:HALF, HALF:] = empty
    li_ref[HALF:, :HALF] = i21
    li_ref[HALF:, HALF:] = i2
    l_ref[:HALF, :HALF] = t_s[0].T
    l_ref[:HALF, HALF:] = empty
    l_ref[HALF:, HALF:] = t_s[2].T
    inverse = li_ref[...]
    for r in range(step + 1, STEPS):
        g = root_rows(root_s, r) + placed(r * PANEL, PANEL, map_ref, step_col)
        for m in range(step):
            g = g - mm_nt(before_a[m][(r - m - 1) * PANEL : (r - m) * PANEL, :], mine(m))
        xa_ref[(r - step - 1) * PANEL : (r - step) * PANEL, :] = mm_nt(g, inverse, HIGHEST).astype(BF16)
    g = root_mine[...].astype(F32)
    g = g + placed(place_ref[0] * device_rows, device_rows, map_ref, step_col)
    for m in range(step):
        g = g - mm_nt(before_r[m][...], mine(m))
    xr_ref[...] = mm_nt(g, inverse, HIGHEST).astype(BF16)
    h = root_rows(rown_s, step) + placed(first, PANEL, map_ref, own_col)
    for m in range(step):
        h = h - mm(mine(m), before_y[m][...])
    y_ref[...] = mm(inverse, h, HIGHEST).astype(BF16)


def last_kernel(leaves, *refs):
    place_ref, map_ref, root_ref = refs[:3]
    refs = refs[3:]
    own_col, refs = refs[:leaves], refs[leaves:]
    xr, refs = refs[:STEPS], refs[STEPS:]
    y, refs = refs[:STEPS], refs[STEPS:]
    factor, refs = refs[:STEPS], refs[STEPS:]
    inverse, refs = refs[:STEPS], refs[STEPS:]
    out_ref, l_s, li_s = refs
    device_rows = out_ref.shape[0]
    panel = place_ref[1]
    base = place_ref[0] * device_rows
    t = root_ref[...] + placed(base, device_rows, map_ref, own_col)
    for m in range(STEPS):
        use = jnp.where(m < panel, 1.0, 0.0).astype(BF16)
        t = t - mm(xr[m][...], y[m][...] * use)
    rows = lax.broadcasted_iota(jnp.int32, (device_rows, 1), 0) + base

    @pl.when(panel >= STEPS)
    def _():
        out_ref[...] = jnp.where(rows >= DONE, t, 0.0)

    for m in range(STEPS):

        @pl.when(panel == m)
        def _():
            l_s[...] = factor[m][...]
            li_s[...] = inverse[m][...]

    @pl.when(panel < STEPS)
    def _():
        below = mm_nt(t, li_s[...], HIGHEST)
        out_ref[...] = jnp.where(rows >= (panel + 1) * PANEL, below, 0.0)
        for half in range(device_rows // PANEL):

            @pl.when(base + half * PANEL == panel * PANEL)
            def _():
                out_ref[half * PANEL : (half + 1) * PANEL, :] = l_s[...]


def flip(value, axis, bits, count):
    return lax.ppermute(value, axis, [(i, i ^ bits) for i in range(count)])


def over_leaf(value, leaf_count):
    found = [value]
    bit = leaf_count // 2
    parts = {0: value}
    order = []
    while bit:
        order.append(bit)
        bit //= 2
    for bit in order:
        for have in list(parts):
            parts[have | bit] = flip(parts[have], "leaf", bit, leaf_count)
    found = [parts[x] for x in range(leaf_count)]
    return found


def per_device(root_entries, child_updates, child_map, tile_pattern):
    device_rows, panel_width = root_entries.shape
    child_cols = child_updates.shape[1]
    leaf_count = lax.axis_size("leaf")
    panel_count = lax.axis_size("panel")
    leaf = lax.axis_index("leaf")
    panel = lax.axis_index("panel")
    child_order = child_cols * panel_count
    half_leaf = leaf_count // 2
    tile_width = child_order // tile_pattern.shape[1]
    tiles = device_rows // tile_width
    child = leaf // half_leaf
    params = pltpu.CompilerParams(vmem_limit_bytes=56 * 2**20)

    high = lax.reduce_precision(root_entries, 8, 7)
    offset = panel * PANEL % device_rows
    rest = lax.dynamic_slice_in_dim(root_entries - high, offset, PANEL, 0)
    column = jnp.concatenate([high.astype(BF16), rest.astype(BF16)], 0)
    root_all = lax.all_gather(column, "panel", axis=0)

    pieces = [child_updates] + [
        flip(child_updates, "panel", k, panel_count) for k in range(1, panel_count)
    ]
    order = panel ^ jnp.arange(panel_count, dtype=jnp.int32)
    own_map = lax.dynamic_index_in_dim(child_map, child, 0, keepdims=False)
    col_map = own_map.reshape(panel_count, child_cols)[order].reshape(1, child_order)
    pattern = lax.dynamic_index_in_dim(tile_pattern, child, 0, keepdims=False)
    mirrored = jnp.maximum(pattern, pattern.T)
    keep = lax.dynamic_slice_in_dim(mirrored, leaf % half_leaf * tiles, tiles, 0)[:, order]
    keep = (keep > 0).astype(jnp.int32)
    bases = jnp.concatenate(
        [jnp.arange(STEPS, dtype=jnp.int32) * PANEL, (panel * PANEL)[None].astype(jnp.int32)]
    )
    picked = pl.pallas_call(
        select_kernel,
        grid=(STEPS + 1,),
        in_specs=[SMEM_SPEC, SMEM_SPEC, VMEM_SPEC] + [VMEM_SPEC] * panel_count,
        out_specs=pl.BlockSpec((1, device_rows, PANEL), lambda b: (b, 0, 0)),
        out_shape=jax.ShapeDtypeStruct((STEPS + 1, device_rows, PANEL), BF16),
        compiler_params=params,
    )(bases, keep, col_map, *pieces)

    leaf_order = leaf ^ jnp.arange(leaf_count, dtype=jnp.int32)
    row_map = child_map.reshape(leaf_count, device_rows)[leaf_order].reshape(1, 2 * child_order)
    own_col = over_leaf(picked[STEPS], leaf_count)
    need = -(-DONE // device_rows)
    spots = leaf_count if leaf_count <= 4 else need
    slots = max(spots, need)
    spot_order = leaf_order if leaf_count <= 4 else jnp.arange(need, dtype=jnp.int32)
    place = jnp.concatenate([jnp.stack([leaf, panel]).astype(jnp.int32), spot_order])

    def root_pieces(value):
        if leaf_count <= 4:
            return over_leaf(value, leaf_count)
        every = lax.all_gather(value, "leaf", axis=0)
        return [every[x] for x in range(need)]

    root_own = root_pieces(high.astype(BF16))

    xa, xr, ys, factors, inverses = [], [], [], [], []
    for step in range(STEPS):
        child_part, root_part = picked[step], root_all[step]
        if step:
            held = xr[-1] if leaf_count > 4 else root_step[-1]
            child_part, root_part, _ = lax.optimization_barrier((child_part, root_part, held))
        step_col = over_leaf(child_part, leaf_count)
        root_step = root_pieces(root_part)
        root_mine = root_part[:device_rows]
        later = STEPS - 1 - step
        shapes = [jax.ShapeDtypeStruct((later * PANEL, PANEL), BF16)] if later else []
        shapes += [
            jax.ShapeDtypeStruct((device_rows, PANEL), BF16),
            jax.ShapeDtypeStruct((PANEL, PANEL), BF16),
            jax.ShapeDtypeStruct((PANEL, PANEL), F32),
            jax.ShapeDtypeStruct((PANEL, PANEL), F32),
        ]
        args = [*own_col, *step_col, *root_own, *root_step, root_mine, *xa, *xr, *ys]
        out = pl.pallas_call(
            functools.partial(step_kernel, step, leaf_count, spots),
            in_specs=[SMEM_SPEC] + [VMEM_SPEC] * (1 + len(args)),
            out_specs=[VMEM_SPEC] * len(shapes),
            out_shape=shapes,
            scratch_shapes=[
                pltpu.VMEM((slots, device_rows + PANEL, PANEL), BF16),
                pltpu.VMEM((slots, device_rows, PANEL), BF16),
                pltpu.VMEM((2, HALF, HALF), F32),
                pltpu.VMEM((4, HALF, HALF), F32),
            ],
            cost_estimate=pl.CostEstimate(
                flops=20 * 10**9, transcendentals=0, bytes_accessed=4 * 2**20
            ),
            compiler_params=params,
        )(place, row_map, *args)
        if later:
            xa.append(out[0])
            out = out[1:]
        xr.append(out[0])
        ys.append(out[1])
        factors.append(out[2])
        inverses.append(out[3])

    args = [root_entries, *own_col, *xr, *ys, *factors, *inverses]
    return pl.pallas_call(
        functools.partial(last_kernel, leaf_count),
        in_specs=[SMEM_SPEC] + [VMEM_SPEC] * (1 + len(args)),
        out_specs=VMEM_SPEC,
        out_shape=jax.ShapeDtypeStruct((device_rows, panel_width), F32),
        scratch_shapes=[pltpu.VMEM((PANEL, PANEL), F32)] * 2,
        compiler_params=params,
    )(place, row_map, *args)


def solution(mesh):
    spots = (P("leaf", "panel"), P("leaf", "panel"), P(), P())
    return jax.shard_map(
        per_device, mesh=mesh, in_specs=spots, out_specs=P("leaf", "panel"), check_vma=False
    )
```

```python
import functools

import jax
import jax.numpy as jnp
from jax import lax
from jax.experimental import pallas as pl
from jax.experimental.pallas import tpu as pltpu
from jax.sharding import PartitionSpec as P

PANEL = 256
STEPS = 5
HALF = PANEL // 2
SUB = 8
BAND = 32
DONE = STEPS * PANEL
HIGHEST = lax.Precision.HIGHEST
F32 = jnp.float32
BF16 = jnp.bfloat16
SMEM_SPEC = pl.BlockSpec(memory_space=pltpu.SMEM)
VMEM_SPEC = pl.BlockSpec(memory_space=pltpu.VMEM)


def mm(a, b, precision=None):
    return lax.dot_general(
        a, b, (((1,), (0,)), ((), ())), precision=precision, preferred_element_type=F32
    )


def mm_nt(a, b, precision=None):
    return lax.dot_general(
        a, b, (((1,), (1,)), ((), ())), precision=precision, preferred_element_type=F32
    )


def thirds(x):
    high = x.astype(BF16)
    rest = x - high.astype(F32)
    middle = rest.astype(BF16)
    return high, middle, (rest - middle.astype(F32)).astype(BF16)


def mm3_nt(a, b):
    ah, bh = a.astype(BF16), b.astype(BF16)
    al, bl = (a - ah.astype(F32)).astype(BF16), (b - bh.astype(F32)).astype(BF16)
    return mm_nt(jnp.concatenate([ah, ah, al], 1), jnp.concatenate([bh, bl, bh], 1))


def mm3(a, b):
    ah, bh = a.astype(BF16), b.astype(BF16)
    al, bl = (a - ah.astype(F32)).astype(BF16), (b - bh.astype(F32)).astype(BF16)
    return mm(jnp.concatenate([ah, ah, al], 1), jnp.concatenate([bh, bl, bh], 0))


def factor_half(a):
    n = a.shape[0]
    groups = BAND // SUB
    lane = lax.broadcasted_iota(jnp.int32, (SUB, n), 1)
    sub = lax.broadcasted_iota(jnp.int32, (SUB, n), 0)
    band_lane = lax.broadcasted_iota(jnp.int32, (BAND, n), 1)
    band_sub = lax.broadcasted_iota(jnp.int32, (BAND, n), 0)

    def full(v):
        return jnp.broadcast_to(v, (SUB, n))

    left = a
    uppers, inverses = [], []
    for base in range(0, n, BAND):
        rows = [left[SUB * g : SUB * g + SUB, :] for g in range(groups)]
        inv = [
            jnp.where(lane < base, rows[g], jnp.where(lane == sub + (base + SUB * g), 1.0, 0.0))
            for g in range(groups)
        ]
        for g in range(groups):
            below = groups - g
            at = base + SUB * g
            col = [
                [full(rows[g + h][:, at + q : at + q + 1]) for h in range(below)] for q in range(SUB)
            ]
            tip = [
                [full(col[q][0][r : r + 1, :]) if r >= q else None for r in range(SUB)]
                for q in range(SUB)
            ]
            for q in range(SUB):
                scale = lax.rsqrt(tip[q][q])
                part = [tip[q][r] * scale if r > q else None for r in range(SUB)]
                for q2 in range(q + 1, SUB):
                    for r in range(q2, SUB):
                        tip[q2][r] = tip[q2][r] - part[r] * part[q2]
                mult = [col[q][h] * scale for h in range(below)]
                mult[0] = jnp.where(sub > q, mult[0], 0.0)
                for q2 in range(q + 1, SUB):
                    for h in range(below):
                        col[q2][h] = col[q2][h] - mult[h] * part[q2]
                for x in (rows, inv):
                    row = full(x[g][q : q + 1, :]) * scale
                    x[g] = jnp.where(sub == q, row, x[g] - mult[0] * row)
                    for h in range(1, below):
                        x[g + h] = x[g + h] - mult[h] * row
        upper = jnp.concatenate(rows, 0)
        inverse = jnp.concatenate(inv, 0)
        uppers.append(jnp.where(band_lane >= band_sub + base, upper, 0.0))
        inverses.append(inverse)
        if base + BAND < n:
            both = jnp.where(band_lane < base + BAND, inverse, upper)
            uh, um, ul = thirds(upper)
            bh, bm, bl = thirds(both)
            product = lax.dot_general(
                jnp.concatenate([uh, uh, um, uh, ul, um], 0),
                jnp.concatenate([bh, bm, bh, bl, bh, bm], 0),
                (((0,), (0,)), ((), ())),
                preferred_element_type=F32,
            )
            left = left[BAND:, :]
            at = lax.broadcasted_iota(jnp.int32, left.shape, 1)
            left = jnp.where((at >= base) & (at < base + BAND), 0.0, left) - product[base + BAND :, :]
    return jnp.concatenate(uppers, 0), jnp.concatenate(inverses, 0)


def select_kernel(bases_ref, keep_ref, map_ref, *refs):
    count = bases_ref.shape[0]
    pieces, outs = refs[:-count], refs[-count:]
    width = pieces[0].shape[1]
    tiles = keep_ref.shape[0]
    tile = pieces[0].shape[0] // tiles
    kept = []
    for k, piece in enumerate(pieces):
        kept.append(
            jnp.concatenate(
                [
                    piece[t * tile : (t + 1) * tile, :] * keep_ref[t, k].astype(F32).astype(BF16)
                    for t in range(tiles)
                ],
                0,
            )
        )
    kept = jnp.concatenate(kept, 1)
    ids = lax.broadcasted_iota(jnp.int32, (PANEL, 1), 0)
    for block in range(count):
        hot = (ids + bases_ref[block] == map_ref[...]).astype(F32).astype(BF16)
        outs[block][...] = mm_nt(kept, hot).astype(BF16)


def placed(row_base, count, map_ref, pieces):
    width = pieces[0].shape[0]
    ids = lax.broadcasted_iota(jnp.int32, (count, 1), 0) + row_base
    total = None
    for x, piece in enumerate(pieces):
        hot = (ids == map_ref[:, x * width : (x + 1) * width]).astype(F32).astype(BF16)
        term = mm(hot, piece[...])
        total = term if total is None else total + term
    return total


def solve_right(g, i1, l21, i2):
    one = mm3_nt(g[:, :HALF], i1)
    two = mm3_nt(g[:, HALF:] - mm3_nt(one, l21), i2)
    return jnp.concatenate([one, two], 1)


def solve_left(h, i1, l21, i2):
    one = mm3(i1, h[:HALF, :])
    two = mm3(i2, h[HALF:, :] - mm3(l21, one))
    return jnp.concatenate([one, two], 0)


def step_kernel(step, leaves, spots, *refs):
    refs = list(refs)

    def take(count):
        out = refs[:count]
        del refs[:count]
        return out

    (place_ref, map_ref) = take(2)
    step_col, root_step, (root_mine,) = take(leaves), take(spots), take(1)
    earlier = max(step - 1, 0)
    if step:
        own_col, root_own = take(leaves), take(spots)
        before_a, before_r, before_y = take(step), take(earlier), take(earlier)
        (sum_ref, rest_ref) = take(2)
        factors = take(step)
    last = step == STEPS - 1
    if last:
        (out_ref,) = take(1)
    else:
        (xa_ref, gr_ref, fac_ref) = take(3)
        if step:
            (xr_ref, y_ref, t_ref) = take(3)
    (root_s,) = take(1)
    if step:
        (rown_s,) = take(1)
    device_rows = step_col[0].shape[0]
    per_leaf = device_rows // PANEL
    panel = place_ref[1]
    base = place_ref[0] * device_rows
    for x in range(spots):
        leaf = place_ref[2 + x]
        root_s[leaf] = root_step[x][...]
        if step:
            rown_s[leaf] = root_own[x][...]

    def root_rows(scratch, r):
        return scratch[r // per_leaf, pl.ds(r % per_leaf * PANEL, PANEL), :].astype(F32)

    def panel_rows(m, r):
        return before_a[m][(r - m - 1) * PANEL : (r - m) * PANEL, :]

    diag = root_rows(root_s, step) + root_s[step // per_leaf, pl.ds(device_rows, PANEL), :].astype(F32)
    diag = diag + placed(step * PANEL, PANEL, map_ref, step_col)
    for m in range(step):
        diag = diag - mm_nt(panel_rows(m, step), panel_rows(m, step))
    t1, i1 = factor_half(diag[:HALF, :HALF])
    below = []
    for r in range(step + 1, STEPS):
        g = root_rows(root_s, r) + placed(r * PANEL, PANEL, map_ref, step_col)
        for m in range(step):
            g = g - mm_nt(panel_rows(m, r), panel_rows(m, step))
        below.append(g)
    mine = root_mine[:device_rows, :].astype(F32) + placed(base, device_rows, map_ref, step_col)
    if step:
        prev = step - 1
        fac = factors[prev]
        p1, pl21, p2 = fac[3], fac[1], fac[4]
        xr_new = solve_right(sum_ref[...], p1, pl21, p2).astype(BF16)
        rows = [before_r[m][...] for m in range(prev)] + [xr_new]
        for m in range(step):
            mine = mine - mm_nt(rows[m], panel_rows(m, step))
        h = root_rows(rown_s, prev) + placed(prev * PANEL, PANEL, map_ref, own_col)
        for m in range(prev):
            h = h - mm(panel_rows(m, prev), before_y[m][...])
        y_new = solve_left(h, p1, pl21, p2).astype(BF16)
        t = rest_ref[...]
        if step == 1:
            t = t + placed(base, device_rows, map_ref, own_col)
        t = t - mm(xr_new, y_new * jnp.where(prev < panel, 1.0, 0.0).astype(BF16))
        if not last:
            xr_ref[...] = xr_new
            y_ref[...] = y_new
            t_ref[...] = t
    if not last:
        gr_ref[...] = mine
    l21 = mm3_nt(diag[HALF:, :HALF], i1)
    t2, i2 = factor_half(diag[HALF:, HALF:] - mm3_nt(l21, l21))
    if not last:
        for n, value in enumerate((t1, l21, t2, i1, i2)):
            fac_ref[n] = value
        g = jnp.concatenate(below, 0)
        one = mm3_nt(g[:, :HALF], i1)
        two = g[:, HALF:] - mm3_nt(one, l21)
        xa_ref[:, :HALF] = one.astype(BF16)
        xa_ref[:, HALF:] = mm3_nt(two, i2).astype(BF16)
        return
    h = root_rows(rown_s, step) + placed(step * PANEL, PANEL, map_ref, own_col)
    for m in range(prev):
        h = h - mm(panel_rows(m, step), before_y[m][...])
    h = h - mm(panel_rows(prev, step), y_new)
    rows = lax.broadcasted_iota(jnp.int32, (device_rows, 1), 0) + base
    fac_s = refs[0]

    @pl.when(panel >= STEPS)
    def _():
        xr = solve_right(mine, i1, l21, i2).astype(BF16)
        y = solve_left(h, i1, l21, i2).astype(BF16)
        out_ref[...] = jnp.where(rows >= DONE, t - mm(xr, y), 0.0)

    for m in range(STEPS - 1):

        @pl.when(panel == m)
        def _():
            fac_s[...] = factors[m][...]

    @pl.when(panel == STEPS - 1)
    def _():
        for n, value in enumerate((t1, l21, t2, i1, i2)):
            fac_s[n] = value

    @pl.when(panel < STEPS)
    def _():
        solved = solve_right(t, fac_s[3], fac_s[1], fac_s[4])
        out_ref[...] = jnp.where(rows >= (panel + 1) * PANEL, solved, 0.0)
        for part in range(device_rows // PANEL):
            start = part * PANEL

            @pl.when(base + start == panel * PANEL)
            def _():
                out_ref[start : start + HALF, :HALF] = fac_s[0].T
                out_ref[start + HALF : start + PANEL, :HALF] = fac_s[1]
                out_ref[start + HALF : start + PANEL, HALF:] = fac_s[2].T


def flip(value, axis, bits, count):
    return lax.ppermute(value, axis, [(i, i ^ bits) for i in range(count)])


def after(value, *held):
    return lax.optimization_barrier((value, *held))[0]


def over_leaf(value, leaf_count, first=None, second=None):
    if first is not None:
        value = after(value, first)
    parts = {0: value}
    bit = leaf_count // 2
    while bit:
        for have in list(parts):
            part = parts[have] if second is None or not have else after(parts[have], second)
            parts[have | bit] = flip(part, "leaf", bit, leaf_count)
        bit //= 2
    return [parts[x] for x in range(leaf_count)]


def over_panel(value, panel_count):
    parts = {0: value}
    bit = panel_count // 2
    while bit > 2:
        for have in list(parts):
            parts[have | bit] = flip(parts[have], "panel", bit, panel_count)
        bit //= 2
    for have in list(parts):
        for near in range(1, 2 * bit):
            parts[have | near] = flip(parts[have], "panel", near, panel_count)
    return [parts[x] for x in range(panel_count)]


def per_device(root_entries, child_updates, child_map, tile_pattern):
    device_rows, panel_width = root_entries.shape
    child_cols = child_updates.shape[1]
    leaf_count = lax.axis_size("leaf")
    panel_count = lax.axis_size("panel")
    leaf = lax.axis_index("leaf")
    panel = lax.axis_index("panel")
    child_order = child_cols * panel_count
    half_leaf = leaf_count // 2
    tile_width = child_order // tile_pattern.shape[1]
    tiles = device_rows // tile_width
    child = leaf // half_leaf
    small = leaf_count == 4 and panel_count == 8
    params = pltpu.CompilerParams(vmem_limit_bytes=56 * 2**20)

    high = lax.reduce_precision(root_entries, 8, 7)
    offset = panel * PANEL % device_rows
    rest = lax.dynamic_slice_in_dim(root_entries - high, offset, PANEL, 0)
    column = jnp.concatenate([high.astype(BF16), rest.astype(BF16)], 0)

    pieces = over_panel(child_updates, panel_count)
    if small:
        columns = over_panel(after(column, pieces[4]), panel_count)
        root_all = jnp.zeros((STEPS + 1, *column.shape), BF16)
        for x in (0, 4, 1, 2, 3, 5, 6, 7):
            slot = jnp.minimum(panel ^ x, STEPS)
            root_all = lax.dynamic_update_slice(root_all, columns[x][None], (slot, 0, 0))
    else:
        root_all = lax.all_gather(column, "panel", axis=0)
    order = panel ^ jnp.arange(panel_count, dtype=jnp.int32)
    own_map = lax.dynamic_index_in_dim(child_map, child, 0, keepdims=False)
    col_map = own_map.reshape(panel_count, child_cols)[order].reshape(1, child_order)
    pattern = lax.dynamic_index_in_dim(tile_pattern, child, 0, keepdims=False)
    mirrored = jnp.maximum(pattern, pattern.T)
    keep = lax.dynamic_slice_in_dim(mirrored, leaf % half_leaf * tiles, tiles, 0)[:, order]
    keep = (keep > 0).astype(jnp.int32)

    def select(bases):
        count = bases.shape[0]
        return pl.pallas_call(
            select_kernel,
            in_specs=[SMEM_SPEC, SMEM_SPEC, VMEM_SPEC] + [VMEM_SPEC] * panel_count,
            out_specs=[VMEM_SPEC] * count,
            out_shape=[jax.ShapeDtypeStruct((device_rows, PANEL), BF16)] * count,
            compiler_params=params,
            cost_estimate=pl.CostEstimate(
                flops=10**9 * count, transcendentals=0, bytes_accessed=2**20
            ),
        )(bases, keep, col_map, *pieces)

    starts = jnp.arange(STEPS, dtype=jnp.int32) * PANEL
    picked = select(starts[:1])
    picked += select(jnp.concatenate([starts[1:], (panel * PANEL)[None].astype(jnp.int32)]))

    leaf_order = leaf ^ jnp.arange(leaf_count, dtype=jnp.int32)
    row_map = child_map.reshape(leaf_count, device_rows)[leaf_order].reshape(1, 2 * child_order)
    need = -(-DONE // device_rows)
    spots = leaf_count if small else need
    slots = max(spots, need)
    spot_order = leaf_order if small else jnp.arange(need, dtype=jnp.int32)
    place = jnp.concatenate([jnp.stack([leaf, panel]).astype(jnp.int32), spot_order])

    def root_pieces(value, first=None, second=None):
        if small:
            return over_leaf(value, leaf_count, first, second)
        every = lax.all_gather(value if first is None else after(value, first), "leaf", axis=0)
        return [every[x] for x in range(need)]

    xa, xr, ys, factors = [], [], [], []
    early = 4 if small else 1
    cols = [over_leaf(picked[step], leaf_count) for step in range(early)]
    if small:
        own_col = over_leaf(picked[STEPS], leaf_count)
        root_own = root_pieces(after(high.astype(BF16), pieces[1]))
        root_all = after(root_all, own_col[-1], *[c[-1] for c in cols])
        roots = [root_pieces(root_all[0])]
    else:
        roots = [root_pieces(root_all[0])]
    done = [roots[0][-1]]
    for step in range(STEPS):
        if step and not small:
            cols.append(over_leaf(after(picked[step], done[-1]), leaf_count))
            roots.append(root_pieces(root_all[step], done[-1]))
        if step == 1 and not small:
            own_part = after(picked[STEPS], done[-1])
            own_col = over_leaf(own_part, leaf_count)
            root_own = root_pieces(high.astype(BF16), own_part)
        root_mine = root_all[step]
        root_step = roots[step]
        step_col = cols[step]
        last = step == STEPS - 1
        args = [*step_col, *root_step, root_mine]
        scratch = [pltpu.VMEM((slots, device_rows + PANEL, PANEL), BF16)]
        if step:
            args += [*own_col, *root_own, *xa, *xr, *ys, mine, rest_block, *factors]
            scratch += [pltpu.VMEM((slots, device_rows, PANEL), BF16)]
        block = jax.ShapeDtypeStruct((device_rows, PANEL), F32)
        if last:
            shapes = [block]
            scratch += [pltpu.VMEM((5, HALF, HALF), F32)]
        else:
            shapes = [
                jax.ShapeDtypeStruct(((STEPS - 1 - step) * PANEL, PANEL), BF16),
                block,
                jax.ShapeDtypeStruct((5, HALF, HALF), F32),
            ]
            if step:
                shapes += [
                    jax.ShapeDtypeStruct((device_rows, PANEL), BF16),
                    jax.ShapeDtypeStruct((PANEL, PANEL), BF16),
                    block,
                ]
        out = pl.pallas_call(
            functools.partial(step_kernel, step, leaf_count, spots),
            in_specs=[SMEM_SPEC] + [VMEM_SPEC] * (1 + len(args)),
            out_specs=[VMEM_SPEC] * len(shapes),
            out_shape=shapes,
            scratch_shapes=scratch,
            compiler_params=params,
            cost_estimate=pl.CostEstimate(
                flops=15 * 10**9, transcendentals=0, bytes_accessed=4 * 2**20
            ),
        )(place, row_map, *args)
        if last:
            return out[0]
        xa.append(out[0])
        mine = out[1]
        factors.append(out[2])
        rest_block = root_entries
        if step:
            xr.append(out[3])
            ys.append(out[4])
            rest_block = out[5]
        done.append(out[0])
        if small and step == 0:
            roots.append(root_pieces(root_all[1], done[0], done[1]))
        elif small and step == 1:
            roots.append(root_pieces(root_all[2], done[0], done[2]))
        if small and 0 < step < STEPS - 2:
            at = step + 2
            cols += [over_leaf(picked[n], leaf_count, done[step], done[step + 1]) for n in range(len(cols), at + 1)]
            roots.append(root_pieces(root_all[at], done[step], done[step + 1]))


def solution(mesh):
    spots = (P("leaf", "panel"), P("leaf", "panel"), P(), P())
    return jax.shard_map(
        per_device, mesh=mesh, in_specs=spots, out_specs=P("leaf", "panel"), check_vma=False
    )
```

```python
import functools

import jax
import jax.numpy as jnp
from jax import lax
from jax.experimental import pallas as pl
from jax.experimental.pallas import tpu as pltpu
from jax.sharding import PartitionSpec as P

PANEL = 256
STEPS = 5
HALF = PANEL // 2
SUB = 8
BAND = 32
DONE = STEPS * PANEL
HIGHEST = lax.Precision.HIGHEST
F32 = jnp.float32
BF16 = jnp.bfloat16
SMEM_SPEC = pl.BlockSpec(memory_space=pltpu.SMEM)
VMEM_SPEC = pl.BlockSpec(memory_space=pltpu.VMEM)


def mm(a, b, precision=None):
    return lax.dot_general(
        a, b, (((1,), (0,)), ((), ())), precision=precision, preferred_element_type=F32
    )


def mm_nt(a, b, precision=None):
    return lax.dot_general(
        a, b, (((1,), (1,)), ((), ())), precision=precision, preferred_element_type=F32
    )


def thirds(x):
    high = x.astype(BF16)
    rest = x - high.astype(F32)
    middle = rest.astype(BF16)
    return high, middle, (rest - middle.astype(F32)).astype(BF16)


def mm3_nt(a, b):
    ah, bh = a.astype(BF16), b.astype(BF16)
    al, bl = (a - ah.astype(F32)).astype(BF16), (b - bh.astype(F32)).astype(BF16)
    return mm_nt(jnp.concatenate([ah, ah, al], 1), jnp.concatenate([bh, bl, bh], 1))


def mm3(a, b):
    ah, bh = a.astype(BF16), b.astype(BF16)
    al, bl = (a - ah.astype(F32)).astype(BF16), (b - bh.astype(F32)).astype(BF16)
    return mm(jnp.concatenate([ah, ah, al], 1), jnp.concatenate([bh, bl, bh], 0))


def factor_half(a):
    n = a.shape[0]
    groups = BAND // SUB
    lane = lax.broadcasted_iota(jnp.int32, (SUB, n), 1)
    sub = lax.broadcasted_iota(jnp.int32, (SUB, n), 0)
    band_lane = lax.broadcasted_iota(jnp.int32, (BAND, n), 1)
    band_sub = lax.broadcasted_iota(jnp.int32, (BAND, n), 0)

    def full(v):
        return jnp.broadcast_to(v, (SUB, n))

    left = a
    uppers, inverses = [], []
    for base in range(0, n, BAND):
        rows = [left[SUB * g : SUB * g + SUB, :] for g in range(groups)]
        inv = [
            jnp.where(lane < base, rows[g], jnp.where(lane == sub + (base + SUB * g), 1.0, 0.0))
            for g in range(groups)
        ]
        for g in range(groups):
            below = groups - g
            at = base + SUB * g
            col = [
                [full(rows[g + h][:, at + q : at + q + 1]) for h in range(below)] for q in range(SUB)
            ]
            tip = [
                [full(col[q][0][r : r + 1, :]) if r >= q else None for r in range(SUB)]
                for q in range(SUB)
            ]
            for q in range(SUB):
                scale = lax.rsqrt(tip[q][q])
                part = [tip[q][r] * scale if r > q else None for r in range(SUB)]
                for q2 in range(q + 1, SUB):
                    for r in range(q2, SUB):
                        tip[q2][r] = tip[q2][r] - part[r] * part[q2]
                mult = [col[q][h] * scale for h in range(below)]
                mult[0] = jnp.where(sub > q, mult[0], 0.0)
                for q2 in range(q + 1, SUB):
                    for h in range(below):
                        col[q2][h] = col[q2][h] - mult[h] * part[q2]
                for x in (rows, inv):
                    row = full(x[g][q : q + 1, :]) * scale
                    x[g] = jnp.where(sub == q, row, x[g] - mult[0] * row)
                    for h in range(1, below):
                        x[g + h] = x[g + h] - mult[h] * row
        upper = jnp.concatenate(rows, 0)
        inverse = jnp.concatenate(inv, 0)
        uppers.append(jnp.where(band_lane >= band_sub + base, upper, 0.0))
        inverses.append(inverse)
        if base + BAND < n:
            both = jnp.where(band_lane < base + BAND, inverse, upper)
            uh, um, ul = thirds(upper)
            bh, bm, bl = thirds(both)
            product = lax.dot_general(
                jnp.concatenate([uh, uh, um, uh, ul, um], 0),
                jnp.concatenate([bh, bm, bh, bl, bh, bm], 0),
                (((0,), (0,)), ((), ())),
                preferred_element_type=F32,
            )
            left = left[BAND:, :]
            at = lax.broadcasted_iota(jnp.int32, left.shape, 1)
            left = jnp.where((at >= base) & (at < base + BAND), 0.0, left) - product[base + BAND :, :]
    return jnp.concatenate(uppers, 0), jnp.concatenate(inverses, 0)


def select_kernel(bases_ref, keep_ref, map_ref, *refs):
    count = bases_ref.shape[0]
    pieces, outs = refs[:-count], refs[-count:]
    width = pieces[0].shape[1]
    tiles = keep_ref.shape[0]
    tile = pieces[0].shape[0] // tiles
    kept = []
    for k, piece in enumerate(pieces):
        kept.append(
            jnp.concatenate(
                [
                    piece[t * tile : (t + 1) * tile, :] * keep_ref[t, k].astype(F32).astype(BF16)
                    for t in range(tiles)
                ],
                0,
            )
        )
    kept = jnp.concatenate(kept, 1)
    ids = lax.broadcasted_iota(jnp.int32, (PANEL, 1), 0)
    for block in range(count):
        hot = (ids + bases_ref[block] == map_ref[...]).astype(F32).astype(BF16)
        outs[block][...] = mm_nt(kept, hot).astype(BF16)


def placed(row_base, count, map_ref, pieces, lanes=slice(None)):
    width = pieces[0].shape[0]
    ids = lax.broadcasted_iota(jnp.int32, (count, 1), 0) + row_base
    total = None
    for x, piece in enumerate(pieces):
        hot = (ids == map_ref[:, x * width : (x + 1) * width]).astype(F32).astype(BF16)
        term = mm(hot, piece[:, lanes])
        total = term if total is None else total + term
    return total


def solve_right(g, i1, l21, i2):
    one = mm3_nt(g[:, :HALF], i1)
    two = mm3_nt(g[:, HALF:] - mm3_nt(one, l21), i2)
    return jnp.concatenate([one, two], 1)


def solve_left(h, i1, l21, i2):
    one = mm3(i1, h[:HALF, :])
    two = mm3(i2, h[HALF:, :] - mm3(l21, one))
    return jnp.concatenate([one, two], 0)


def step_kernel(step, leaves, spots, *refs):
    refs = list(refs)

    def take(count):
        out = refs[:count]
        del refs[:count]
        return out

    (place_ref, map_ref) = take(2)
    step_col, root_step, (root_mine,) = take(leaves), take(spots), take(1)
    prev = step - 1
    last = step == STEPS - 1
    if step:
        own_col, root_own = take(leaves), take(spots)
        before_a, before_r, before_y = take(step), take(prev), take(prev)
        (sum_ref, rest_ref) = take(2)
        factors = take(step)
    if last:
        (out_ref,) = take(1)
        (fac_ref, gr_ref, xr_ref, y_ref, t_ref, h_ref) = refs[-6:]
    else:
        (xa_ref, gr_ref, fac_ref) = take(3)
        if step:
            (xr_ref, y_ref, t_ref) = take(3)
    (root_s, d_s) = take(2)
    if step:
        (rown_s,) = take(1)
    if not last:
        (g_s,) = take(1)
    device_rows = step_col[0].shape[0]
    per_leaf = device_rows // PANEL
    panel = place_ref[1]
    base = place_ref[0] * device_rows
    for x in range(spots):
        leaf = place_ref[2 + x]
        root_s[leaf] = root_step[x][...]
        if step:
            rown_s[leaf] = root_own[x][...]

    def panel_rows(m, r):
        return before_a[m][(r - m - 1) * PANEL : (r - m) * PANEL, :]

    def own_rows(r, lanes):
        return rown_s[r // per_leaf, pl.ds(r % per_leaf * PANEL, PANEL), lanes].astype(F32)

    share = root_s.shape[1] - device_rows
    if share == PANEL:
        rest = root_s[step // per_leaf, pl.ds(device_rows, PANEL), :]
    else:
        rest = jnp.concatenate(
            [root_s[x, pl.ds(device_rows, share), :] for x in range(PANEL // share)], 0
        )
    diag = root_s[step // per_leaf, pl.ds(step % per_leaf * PANEL, PANEL), :].astype(F32)
    diag = diag + rest.astype(F32) + placed(step * PANEL, PANEL, map_ref, step_col)
    for m in range(step):
        diag = diag - mm_nt(panel_rows(m, step), panel_rows(m, step))
    d_s[0] = diag[:HALF, :HALF]
    d_s[1] = diag[HALF:, HALF:]
    fac_ref[1] = diag[HALF:, :HALF]
    pieces = STEPS - 1 - step
    part = device_rows // 2

    def half(n, carry):
        upper, inverse = factor_half(d_s[n])
        fac_ref[2 * n] = upper
        fac_ref[3 + n] = inverse
        if not last:
            count = pieces * HALF
            here = pl.ds(pl.multiple_of(n * count, HALF), count)
            start = (step + 1) * PANEL + n * count
            found = []
            for c in range(pieces):
                row = start + c * HALF
                at = pl.ds(pl.multiple_of(row % device_rows, HALF), HALF)
                found.append(root_s[row // device_rows, at, :])
            g = jnp.concatenate(found, 0).astype(F32) + placed(start, count, map_ref, step_col)
            for m in range(step):
                at = pl.ds(pl.multiple_of((step - m) * PANEL + n * count, HALF), count)
                g = g - mm_nt(before_a[m][at, :], panel_rows(m, step))
            g_s[here, :] = g
        rows = pl.ds(pl.multiple_of(n * part, HALF), part)
        mine = root_mine[rows, :].astype(F32) + placed(base + n * part, part, map_ref, step_col)
        if step:
            fac = factors[prev]
            p1, pl21, p2 = fac[3], fac[1], fac[4]
            xr = solve_right(sum_ref[rows, :], p1, pl21, p2).astype(BF16)
            for m in range(prev):
                mine = mine - mm_nt(before_r[m][rows, :], panel_rows(m, step))
            mine = mine - mm_nt(xr, panel_rows(prev, step))
            xr_ref[rows, :] = xr
            lanes = pl.ds(pl.multiple_of(n * HALF, HALF), HALF)
            h = own_rows(prev, lanes) + placed(prev * PANEL, PANEL, map_ref, own_col, lanes)
            for m in range(prev):
                h = h - mm(panel_rows(m, prev), before_y[m][:, lanes])
            y = solve_left(h, p1, pl21, p2).astype(BF16)
            y_ref[:, lanes] = y
            t = rest_ref[rows, :]
            if step == 1:
                t = t + placed(base + n * part, part, map_ref, own_col)
            else:
                use = jnp.where(step - 2 < panel, 1.0, 0.0).astype(BF16)
                t = t - mm(before_r[step - 2][rows, :], before_y[step - 2][...] * use)
            t_ref[rows, :] = t
            if last:
                h = own_rows(step, lanes) + placed(step * PANEL, PANEL, map_ref, own_col, lanes)
                for m in range(prev):
                    h = h - mm(panel_rows(m, step), before_y[m][:, lanes])
                h_ref[:, lanes] = h - mm(panel_rows(prev, step), y)
        gr_ref[rows, :] = mine

        @pl.when(n == 0)
        def _():
            low = mm3_nt(fac_ref[1], inverse)
            fac_ref[1] = low
            d_s[1] = d_s[1] - mm3_nt(low, low)

        return carry

    lax.fori_loop(0, 2, half, 0)
    l21, i1, i2 = fac_ref[1], fac_ref[3], fac_ref[4]
    if not last:
        xa_ref[...] = solve_right(g_s[...], i1, l21, i2).astype(BF16)
        return
    rows = lax.broadcasted_iota(jnp.int32, (device_rows, 1), 0) + base
    use = jnp.where(prev < panel, 1.0, 0.0).astype(BF16)
    t = t_ref[...] - mm(xr_ref[...], y_ref[...] * use)

    @pl.when(panel >= STEPS)
    def _():
        xr = solve_right(gr_ref[...], i1, l21, i2).astype(BF16)
        y = solve_left(h_ref[...], i1, l21, i2).astype(BF16)
        out_ref[...] = jnp.where(rows >= DONE, t - mm(xr, y), 0.0)

    for m in range(STEPS - 1):

        @pl.when(panel == m)
        def _():
            fac_ref[...] = factors[m][...]

    @pl.when(panel < STEPS)
    def _():
        solved = solve_right(t, fac_ref[3], fac_ref[1], fac_ref[4])
        out_ref[...] = jnp.where(rows >= (panel + 1) * PANEL, solved, 0.0)
        for part in range(device_rows // PANEL):
            start = part * PANEL

            @pl.when(base + start == panel * PANEL)
            def _():
                out_ref[start : start + HALF, :HALF] = fac_ref[0].T
                out_ref[start + HALF : start + PANEL, :HALF] = fac_ref[1]
                out_ref[start + HALF : start + PANEL, HALF:] = fac_ref[2].T


def flip(value, axis, bits, count):
    return lax.ppermute(value, axis, [(i, i ^ bits) for i in range(count)])


def after(value, *held):
    return lax.optimization_barrier((value, *held))[0]


def over_leaf(value, leaf_count, first=None, second=None):
    if first is not None:
        value = after(value, first)
    parts = {0: value}
    bit = leaf_count // 2
    while bit:
        for have in list(parts):
            part = parts[have] if second is None or not have else after(parts[have], second)
            parts[have | bit] = flip(part, "leaf", bit, leaf_count)
        bit //= 2
    return [parts[x] for x in range(leaf_count)]


def over_panel(value, panel_count):
    parts = {0: value}
    bit = panel_count // 2
    while bit > 2:
        for have in list(parts):
            parts[have | bit] = flip(parts[have], "panel", bit, panel_count)
        bit //= 2
    for have in list(parts):
        for near in range(1, 2 * bit):
            parts[have | near] = flip(parts[have], "panel", near, panel_count)
    return [parts[x] for x in range(panel_count)]


def per_device(root_entries, child_updates, child_map, tile_pattern):
    device_rows, panel_width = root_entries.shape
    child_cols = child_updates.shape[1]
    leaf_count = lax.axis_size("leaf")
    panel_count = lax.axis_size("panel")
    leaf = lax.axis_index("leaf")
    panel = lax.axis_index("panel")
    child_order = child_cols * panel_count
    half_leaf = leaf_count // 2
    tile_width = child_order // tile_pattern.shape[1]
    tiles = device_rows // tile_width
    child = leaf // half_leaf
    small = leaf_count == 4 and panel_count == 8
    params = pltpu.CompilerParams(vmem_limit_bytes=56 * 2**20)

    high = lax.reduce_precision(root_entries, 8, 7)
    offset = panel * PANEL % device_rows
    rest = lax.dynamic_slice_in_dim(root_entries - high, offset, PANEL, 0)
    rest = rest.astype(BF16)
    if small:
        share = PANEL // leaf_count
        holder = jnp.minimum(panel * PANEL // device_rows, leaf_count - 1)
        shares = [
            lax.dynamic_slice_in_dim(rest, (leaf ^ x) * share, share, 0) for x in range(leaf_count)
        ]
        shares = shares[:1] + [flip(shares[x], "leaf", x, leaf_count) for x in range(1, leaf_count)]
        rest = shares[0]
        for x in range(1, leaf_count):
            rest = jnp.where(leaf ^ x == holder, shares[x], rest)
    column = jnp.concatenate([high.astype(BF16), rest], 0)

    pieces = over_panel(child_updates, panel_count)
    if small:
        columns = over_panel(after(column, pieces[4]), panel_count)
        root_all = jnp.zeros((STEPS + 1, *column.shape), BF16)
        for x in (0, 4, 1, 2, 3, 5, 6, 7):
            slot = jnp.minimum(panel ^ x, STEPS)
            root_all = lax.dynamic_update_slice(root_all, columns[x][None], (slot, 0, 0))
    else:
        root_all = lax.all_gather(column, "panel", axis=0)
    order = panel ^ jnp.arange(panel_count, dtype=jnp.int32)
    own_map = lax.dynamic_index_in_dim(child_map, child, 0, keepdims=False)
    col_map = own_map.reshape(panel_count, child_cols)[order].reshape(1, child_order)
    pattern = lax.dynamic_index_in_dim(tile_pattern, child, 0, keepdims=False)
    mirrored = jnp.maximum(pattern, pattern.T)
    keep = lax.dynamic_slice_in_dim(mirrored, leaf % half_leaf * tiles, tiles, 0)[:, order]
    keep = (keep > 0).astype(jnp.int32)

    def select(bases):
        count = bases.shape[0]
        return pl.pallas_call(
            select_kernel,
            in_specs=[SMEM_SPEC, SMEM_SPEC, VMEM_SPEC] + [VMEM_SPEC] * panel_count,
            out_specs=[VMEM_SPEC] * count,
            out_shape=[jax.ShapeDtypeStruct((device_rows, PANEL), BF16)] * count,
            compiler_params=params,
            cost_estimate=pl.CostEstimate(
                flops=10**9 * count, transcendentals=0, bytes_accessed=2**20
            ),
        )(bases, keep, col_map, *pieces)

    starts = jnp.arange(STEPS, dtype=jnp.int32) * PANEL
    picked = select(starts[:1])
    picked += select(jnp.concatenate([starts[1:], (panel * PANEL)[None].astype(jnp.int32)]))

    leaf_order = leaf ^ jnp.arange(leaf_count, dtype=jnp.int32)
    row_map = child_map.reshape(leaf_count, device_rows)[leaf_order].reshape(1, 2 * child_order)
    need = -(-DONE // device_rows)
    spots = leaf_count if small else need
    slots = max(spots, need)
    spot_order = leaf_order if small else jnp.arange(need, dtype=jnp.int32)
    place = jnp.concatenate([jnp.stack([leaf, panel]).astype(jnp.int32), spot_order])

    def root_pieces(value, first=None, second=None):
        if small:
            return over_leaf(value, leaf_count, first, second)
        every = lax.all_gather(value if first is None else after(value, first), "leaf", axis=0)
        return [every[x] for x in range(need)]

    xa, xr, ys, factors = [], [], [], []
    early = 2 if small else 1
    cols = [over_leaf(picked[step], leaf_count) for step in range(early)]
    if small:
        own_col = over_leaf(picked[STEPS], leaf_count)
        root_own = root_pieces(after(high.astype(BF16), pieces[1]))
        root_all = after(root_all, row_map, place, own_col[-1], *[c[-1] for c in cols])
        roots = [root_pieces(root_all[0])]
    else:
        roots = [root_pieces(root_all[0])]
    done = [roots[0][-1]]
    for step in range(STEPS):
        if step and not small:
            cols.append(over_leaf(after(picked[step], done[-1]), leaf_count))
            roots.append(root_pieces(root_all[step], done[-1]))
        if step == 1 and not small:
            own_part = after(picked[STEPS], done[-1])
            own_col = over_leaf(own_part, leaf_count)
            root_own = root_pieces(high.astype(BF16), own_part)
        root_mine = root_all[step]
        root_step = roots[step]
        step_col = cols[step]
        last = step == STEPS - 1
        args = [*step_col, *root_step, root_mine]
        scratch = [
            pltpu.VMEM((slots, column.shape[0], PANEL), BF16),
            pltpu.VMEM((2, HALF, HALF), F32),
        ]
        if step:
            args += [*own_col, *root_own, *xa, *xr, *ys, mine, rest_block, *factors]
            scratch += [pltpu.VMEM((slots, device_rows, PANEL), BF16)]
        block = jax.ShapeDtypeStruct((device_rows, PANEL), F32)
        if last:
            shapes = [block]
            scratch += [
                pltpu.VMEM((5, HALF, HALF), F32),
                pltpu.VMEM((device_rows, PANEL), F32),
                pltpu.VMEM((device_rows, PANEL), BF16),
                pltpu.VMEM((PANEL, PANEL), BF16),
                pltpu.VMEM((device_rows, PANEL), F32),
                pltpu.VMEM((PANEL, PANEL), F32),
            ]
        else:
            scratch += [pltpu.VMEM(((STEPS - 1 - step) * PANEL, PANEL), F32)]
            shapes = [
                jax.ShapeDtypeStruct(((STEPS - 1 - step) * PANEL, PANEL), BF16),
                block,
                jax.ShapeDtypeStruct((5, HALF, HALF), F32),
            ]
            if step:
                shapes += [
                    jax.ShapeDtypeStruct((device_rows, PANEL), BF16),
                    jax.ShapeDtypeStruct((PANEL, PANEL), BF16),
                    block,
                ]
        out = pl.pallas_call(
            functools.partial(step_kernel, step, leaf_count, spots),
            in_specs=[SMEM_SPEC] + [VMEM_SPEC] * (1 + len(args)),
            out_specs=[VMEM_SPEC] * len(shapes),
            out_shape=shapes,
            scratch_shapes=scratch,
            compiler_params=params,
            cost_estimate=pl.CostEstimate(
                flops=15 * 10**9, transcendentals=0, bytes_accessed=4 * 2**20
            ),
        )(place, row_map, *args)
        if last:
            return out[0]
        xa.append(out[0])
        mine = out[1]
        factors.append(out[2])
        rest_block = root_entries
        if step:
            xr.append(out[3])
            ys.append(out[4])
            rest_block = out[5]
        done.append(out[0])
        if small and not last:
            if step + 2 < STEPS:
                cols.append(over_leaf(picked[step + 2], leaf_count, done[step], done[step + 1]))
            roots.append(root_pieces(root_all[step + 1], done[step], done[step + 1]))


def solution(mesh):
    spots = (P("leaf", "panel"), P("leaf", "panel"), P(), P())
    return jax.shard_map(
        per_device, mesh=mesh, in_specs=spots, out_specs=P("leaf", "panel"), check_vma=False
    )
```

```python
import functools

import jax
import jax.numpy as jnp
from jax import lax
from jax.experimental import pallas as pl
from jax.experimental.pallas import tpu as pltpu
from jax.sharding import PartitionSpec as P

PANEL = 256
STEPS = 5
HALF = PANEL // 2
SUB = 8
BAND = 32
DONE = STEPS * PANEL
HIGHEST = lax.Precision.HIGHEST
F32 = jnp.float32
BF16 = jnp.bfloat16
SMEM_SPEC = pl.BlockSpec(memory_space=pltpu.SMEM)
VMEM_SPEC = pl.BlockSpec(memory_space=pltpu.VMEM)


def mm(a, b, precision=None):
    return lax.dot_general(
        a, b, (((1,), (0,)), ((), ())), precision=precision, preferred_element_type=F32
    )


def mm_nt(a, b, precision=None):
    return lax.dot_general(
        a, b, (((1,), (1,)), ((), ())), precision=precision, preferred_element_type=F32
    )


def thirds(x):
    high = x.astype(BF16)
    rest = x - high.astype(F32)
    middle = rest.astype(BF16)
    return high, middle, (rest - middle.astype(F32)).astype(BF16)


def mm3_nt(a, b):
    ah, bh = a.astype(BF16), b.astype(BF16)
    al, bl = (a - ah.astype(F32)).astype(BF16), (b - bh.astype(F32)).astype(BF16)
    return mm_nt(jnp.concatenate([ah, ah, al], 1), jnp.concatenate([bh, bl, bh], 1))


def mm3(a, b):
    ah, bh = a.astype(BF16), b.astype(BF16)
    al, bl = (a - ah.astype(F32)).astype(BF16), (b - bh.astype(F32)).astype(BF16)
    return mm(jnp.concatenate([ah, ah, al], 1), jnp.concatenate([bh, bl, bh], 0))


def factor_half(a):
    n = a.shape[0]
    groups = BAND // SUB
    lane = lax.broadcasted_iota(jnp.int32, (SUB, n), 1)
    sub = lax.broadcasted_iota(jnp.int32, (SUB, n), 0)
    band_lane = lax.broadcasted_iota(jnp.int32, (BAND, n), 1)
    band_sub = lax.broadcasted_iota(jnp.int32, (BAND, n), 0)

    def full(v):
        return jnp.broadcast_to(v, (SUB, n))

    left = a
    uppers, inverses = [], []
    for base in range(0, n, BAND):
        rows = [left[SUB * g : SUB * g + SUB, :] for g in range(groups)]
        inv = [
            jnp.where(lane < base, rows[g], jnp.where(lane == sub + (base + SUB * g), 1.0, 0.0))
            for g in range(groups)
        ]
        for g in range(groups):
            below = groups - g
            at = base + SUB * g
            col = [
                [full(rows[g + h][:, at + q : at + q + 1]) for h in range(below)] for q in range(SUB)
            ]
            tip = [
                [full(col[q][0][r : r + 1, :]) if r >= q else None for r in range(SUB)]
                for q in range(SUB)
            ]
            for q in range(SUB):
                scale = lax.rsqrt(tip[q][q])
                part = [tip[q][r] * scale if r > q else None for r in range(SUB)]
                for q2 in range(q + 1, SUB):
                    for r in range(q2, SUB):
                        tip[q2][r] = tip[q2][r] - part[r] * part[q2]
                mult = [col[q][h] * scale for h in range(below)]
                mult[0] = jnp.where(sub > q, mult[0], 0.0)
                for q2 in range(q + 1, SUB):
                    for h in range(below):
                        col[q2][h] = col[q2][h] - mult[h] * part[q2]
                for x in (rows, inv):
                    row = full(x[g][q : q + 1, :]) * scale
                    x[g] = jnp.where(sub == q, row, x[g] - mult[0] * row)
                    for h in range(1, below):
                        x[g + h] = x[g + h] - mult[h] * row
        upper = jnp.concatenate(rows, 0)
        inverse = jnp.concatenate(inv, 0)
        uppers.append(jnp.where(band_lane >= band_sub + base, upper, 0.0))
        inverses.append(inverse)
        if base + BAND < n:
            both = jnp.where(band_lane < base + BAND, inverse, upper)
            uh, um, ul = thirds(upper)
            bh, bm, bl = thirds(both)
            product = lax.dot_general(
                jnp.concatenate([uh, uh, um, uh, ul, um], 0),
                jnp.concatenate([bh, bm, bh, bl, bh, bm], 0),
                (((0,), (0,)), ((), ())),
                preferred_element_type=F32,
            )
            left = left[BAND:, :]
            at = lax.broadcasted_iota(jnp.int32, left.shape, 1)
            left = jnp.where((at >= base) & (at < base + BAND), 0.0, left) - product[base + BAND :, :]
    return jnp.concatenate(uppers, 0), jnp.concatenate(inverses, 0)


def select_kernel(bases_ref, keep_ref, map_ref, *refs):
    count = bases_ref.shape[0]
    pieces, outs = refs[:-count], refs[-count:]
    width = pieces[0].shape[1]
    tiles = keep_ref.shape[0]
    tile = pieces[0].shape[0] // tiles
    kept = []
    for k, piece in enumerate(pieces):
        kept.append(
            jnp.concatenate(
                [
                    piece[t * tile : (t + 1) * tile, :] * keep_ref[t, k].astype(F32).astype(BF16)
                    for t in range(tiles)
                ],
                0,
            )
        )
    kept = jnp.concatenate(kept, 1)
    ids = lax.broadcasted_iota(jnp.int32, (PANEL, 1), 0)
    for block in range(count):
        hot = (ids + bases_ref[block] == map_ref[...]).astype(F32).astype(BF16)
        outs[block][...] = mm_nt(kept, hot).astype(BF16)


def placed(row_base, count, map_ref, pieces, lanes=slice(None)):
    width = pieces[0].shape[0]
    ids = lax.broadcasted_iota(jnp.int32, (count, 1), 0) + row_base
    total = None
    for x, piece in enumerate(pieces):
        hot = (ids == map_ref[:, x * width : (x + 1) * width]).astype(F32).astype(BF16)
        term = mm(hot, piece[:, lanes])
        total = term if total is None else total + term
    return total


def solve_right(g, i1, l21, i2):
    one = mm3_nt(g[:, :HALF], i1)
    two = mm3_nt(g[:, HALF:] - mm3_nt(one, l21), i2)
    return jnp.concatenate([one, two], 1)


def solve_left(h, i1, l21, i2):
    one = mm3(i1, h[:HALF, :])
    two = mm3(i2, h[HALF:, :] - mm3(l21, one))
    return jnp.concatenate([one, two], 0)


def step_kernel(step, leaves, spots, *refs):
    refs = list(refs)

    def take(count):
        out = refs[:count]
        del refs[:count]
        return out

    (place_ref, map_ref) = take(2)
    step_col, root_step, (root_mine,) = take(leaves), take(spots), take(1)
    prev = step - 1
    last = step == STEPS - 1
    if step:
        own_col, root_own = take(leaves), take(spots)
        before_a, before_r, before_y = take(step), take(prev), take(prev)
        (sum_ref, rest_ref) = take(2)
        factors = take(step)
    if last:
        (out_ref,) = take(1)
        (fac_ref, gr_ref, xr_ref, y_ref, t_ref, h_ref) = refs[-6:]
    else:
        (xa_ref, gr_ref, fac_ref) = take(3)
        if step:
            (xr_ref, y_ref, t_ref) = take(3)
    (root_s, d_s) = take(2)
    if step:
        (rown_s,) = take(1)
    if not last:
        (g_s,) = take(1)
    device_rows = step_col[0].shape[0]
    per_leaf = device_rows // PANEL
    panel = place_ref[1]
    base = place_ref[0] * device_rows
    for x in range(spots):
        leaf = place_ref[2 + x]
        root_s[leaf] = root_step[x][...]
        if step:
            rown_s[leaf] = root_own[x][...]

    def panel_rows(m, r):
        return before_a[m][(r - m - 1) * PANEL : (r - m) * PANEL, :]

    def own_rows(r, lanes):
        return rown_s[r // per_leaf, pl.ds(r % per_leaf * PANEL, PANEL), lanes].astype(F32)

    share = root_s.shape[1] - device_rows
    if share == PANEL:
        rest = root_s[step // per_leaf, pl.ds(device_rows, PANEL), :]
    else:
        rest = jnp.concatenate(
            [root_s[x, pl.ds(device_rows, share), :] for x in range(PANEL // share)], 0
        )
    diag = root_s[step // per_leaf, pl.ds(step % per_leaf * PANEL, PANEL), :].astype(F32)
    diag = diag + rest.astype(F32) + placed(step * PANEL, PANEL, map_ref, step_col)
    for m in range(step):
        diag = diag - mm_nt(panel_rows(m, step), panel_rows(m, step))
    d_s[0] = diag[:HALF, :HALF]
    d_s[1] = diag[HALF:, HALF:]
    fac_ref[1] = diag[HALF:, :HALF]
    pieces = STEPS - 1 - step
    part = device_rows // 2

    def half(n, carry):
        upper, inverse = factor_half(d_s[n])
        fac_ref[2 * n] = upper
        fac_ref[3 + n] = inverse
        if not last:
            count = pieces * HALF
            here = pl.ds(pl.multiple_of(n * count, HALF), count)
            start = (step + 1) * PANEL + n * count
            found = []
            for c in range(pieces):
                row = start + c * HALF
                at = pl.ds(pl.multiple_of(row % device_rows, HALF), HALF)
                found.append(root_s[row // device_rows, at, :])
            g = jnp.concatenate(found, 0).astype(F32) + placed(start, count, map_ref, step_col)
            for m in range(step):
                at = pl.ds(pl.multiple_of((step - m) * PANEL + n * count, HALF), count)
                g = g - mm_nt(before_a[m][at, :], panel_rows(m, step))
            g_s[here, :] = g
        rows = pl.ds(pl.multiple_of(n * part, HALF), part)
        mine = root_mine[rows, :].astype(F32) + placed(base + n * part, part, map_ref, step_col)
        if step:
            fac = factors[prev]
            p1, pl21, p2 = fac[3], fac[1], fac[4]
            xr = solve_right(sum_ref[rows, :], p1, pl21, p2).astype(BF16)
            for m in range(prev):
                mine = mine - mm_nt(before_r[m][rows, :], panel_rows(m, step))
            mine = mine - mm_nt(xr, panel_rows(prev, step))
            xr_ref[rows, :] = xr
            lanes = pl.ds(pl.multiple_of(n * HALF, HALF), HALF)
            h = own_rows(prev, lanes) + placed(prev * PANEL, PANEL, map_ref, own_col, lanes)
            for m in range(prev):
                h = h - mm(panel_rows(m, prev), before_y[m][:, lanes])
            y = solve_left(h, p1, pl21, p2).astype(BF16)
            y_ref[:, lanes] = y
            t = rest_ref[rows, :]
            if step == 1:
                t = t + placed(base + n * part, part, map_ref, own_col)
            else:
                use = jnp.where(step - 2 < panel, 1.0, 0.0).astype(BF16)
                t = t - mm(before_r[step - 2][rows, :], before_y[step - 2][...] * use)
            t_ref[rows, :] = t
            if last:
                h = own_rows(step, lanes) + placed(step * PANEL, PANEL, map_ref, own_col, lanes)
                for m in range(prev):
                    h = h - mm(panel_rows(m, step), before_y[m][:, lanes])
                h_ref[:, lanes] = h - mm(panel_rows(prev, step), y)
        gr_ref[rows, :] = mine

        @pl.when(n == 0)
        def _():
            low = mm3_nt(fac_ref[1], inverse)
            fac_ref[1] = low
            d_s[1] = d_s[1] - mm3_nt(low, low)

        return carry

    lax.fori_loop(0, 2, half, 0)
    l21, i1, i2 = fac_ref[1], fac_ref[3], fac_ref[4]
    if not last:
        xa_ref[...] = solve_right(g_s[...], i1, l21, i2).astype(BF16)
        return
    rows = lax.broadcasted_iota(jnp.int32, (device_rows, 1), 0) + base
    use = jnp.where(prev < panel, 1.0, 0.0).astype(BF16)
    t = t_ref[...] - mm(xr_ref[...], y_ref[...] * use)

    @pl.when(panel >= STEPS)
    def _():
        xr = solve_right(gr_ref[...], i1, l21, i2).astype(BF16)
        y = solve_left(h_ref[...], i1, l21, i2).astype(BF16)
        out_ref[...] = jnp.where(rows >= DONE, t - mm(xr, y), 0.0)

    for m in range(STEPS - 1):

        @pl.when(panel == m)
        def _():
            fac_ref[...] = factors[m][...]

    @pl.when(panel < STEPS)
    def _():
        solved = solve_right(t, fac_ref[3], fac_ref[1], fac_ref[4])
        out_ref[...] = jnp.where(rows >= (panel + 1) * PANEL, solved, 0.0)
        for part in range(device_rows // PANEL):
            start = part * PANEL

            @pl.when(base + start == panel * PANEL)
            def _():
                out_ref[start : start + HALF, :HALF] = fac_ref[0].T
                out_ref[start + HALF : start + PANEL, :HALF] = fac_ref[1]
                out_ref[start + HALF : start + PANEL, HALF:] = fac_ref[2].T


def flip(value, axis, bits, count):
    return lax.ppermute(value, axis, [(i, i ^ bits) for i in range(count)])


def after(value, *held):
    return lax.optimization_barrier((value, *held))[0]


def over_leaf(value, leaf_count, first=None, second=None):
    if first is not None:
        value = after(value, first)
    parts = {0: value}
    bit = leaf_count // 2
    while bit:
        for have in list(parts):
            part = parts[have] if second is None or not have else after(parts[have], second)
            parts[have | bit] = flip(part, "leaf", bit, leaf_count)
        bit //= 2
    return [parts[x] for x in range(leaf_count)]


def over_panel(value, panel_count):
    parts = {0: value}
    bit = panel_count // 2
    while bit > 2:
        for have in list(parts):
            parts[have | bit] = flip(parts[have], "panel", bit, panel_count)
        bit //= 2
    for have in list(parts):
        for near in range(1, 2 * bit):
            parts[have | near] = flip(parts[have], "panel", near, panel_count)
    return [parts[x] for x in range(panel_count)]


def per_device(root_entries, child_updates, child_map, tile_pattern):
    device_rows, panel_width = root_entries.shape
    child_cols = child_updates.shape[1]
    leaf_count = lax.axis_size("leaf")
    panel_count = lax.axis_size("panel")
    leaf = lax.axis_index("leaf")
    panel = lax.axis_index("panel")
    child_order = child_cols * panel_count
    half_leaf = leaf_count // 2
    tile_width = child_order // tile_pattern.shape[1]
    tiles = device_rows // tile_width
    child = leaf // half_leaf
    small = leaf_count == 4 and panel_count == 8
    params = pltpu.CompilerParams(vmem_limit_bytes=(20 if small else 56) * 2**20)

    def near(x):
        return pltpu.with_memory_space_constraint(x, pltpu.VMEM) if small else x

    high = lax.reduce_precision(root_entries, 8, 7)
    offset = panel * PANEL % device_rows
    rest = lax.dynamic_slice_in_dim(root_entries - high, offset, PANEL, 0)
    rest = rest.astype(BF16)
    if small:
        share = PANEL // leaf_count
        holder = jnp.minimum(panel * PANEL // device_rows, leaf_count - 1)
        shares = [
            lax.dynamic_slice_in_dim(rest, (leaf ^ x) * share, share, 0) for x in range(leaf_count)
        ]
        shares = shares[:1] + [flip(shares[x], "leaf", x, leaf_count) for x in range(1, leaf_count)]
        rest = shares[0]
        for x in range(1, leaf_count):
            rest = jnp.where(leaf ^ x == holder, shares[x], rest)
    column = jnp.concatenate([high.astype(BF16), rest], 0)

    pieces = over_panel(child_updates, panel_count)
    if small:
        columns = over_panel(after(column, pieces[4]), panel_count)
        root_all = jnp.zeros((STEPS + 1, *column.shape), BF16)
        for x in (0, 4, 1, 2, 3, 5, 6, 7):
            slot = jnp.minimum(panel ^ x, STEPS)
            root_all = lax.dynamic_update_slice(root_all, columns[x][None], (slot, 0, 0))
    else:
        root_all = lax.all_gather(column, "panel", axis=0)
    order = panel ^ jnp.arange(panel_count, dtype=jnp.int32)
    own_map = lax.dynamic_index_in_dim(child_map, child, 0, keepdims=False)
    col_map = own_map.reshape(panel_count, child_cols)[order].reshape(1, child_order)
    pattern = lax.dynamic_index_in_dim(tile_pattern, child, 0, keepdims=False)
    mirrored = jnp.maximum(pattern, pattern.T)
    keep = lax.dynamic_slice_in_dim(mirrored, leaf % half_leaf * tiles, tiles, 0)[:, order]
    keep = (keep > 0).astype(jnp.int32)

    def select(bases):
        count = bases.shape[0]
        return pl.pallas_call(
            select_kernel,
            in_specs=[SMEM_SPEC, SMEM_SPEC, VMEM_SPEC] + [VMEM_SPEC] * panel_count,
            out_specs=[VMEM_SPEC] * count,
            out_shape=[jax.ShapeDtypeStruct((device_rows, PANEL), BF16)] * count,
            compiler_params=params,
            cost_estimate=pl.CostEstimate(
                flops=10**9 * count, transcendentals=0, bytes_accessed=2**20
            ),
        )(bases, keep, col_map, *pieces)

    starts = jnp.arange(STEPS, dtype=jnp.int32) * PANEL
    picked = select(starts[:1])
    picked += select(jnp.concatenate([starts[1:], (panel * PANEL)[None].astype(jnp.int32)]))

    leaf_order = leaf ^ jnp.arange(leaf_count, dtype=jnp.int32)
    row_map = child_map.reshape(leaf_count, device_rows)[leaf_order].reshape(1, 2 * child_order)
    need = -(-DONE // device_rows)
    spots = leaf_count if small else need
    slots = max(spots, need)
    spot_order = leaf_order if small else jnp.arange(need, dtype=jnp.int32)
    place = jnp.concatenate([jnp.stack([leaf, panel]).astype(jnp.int32), spot_order])

    def root_pieces(value, first=None, second=None):
        if small:
            return over_leaf(value, leaf_count, first, second)
        every = lax.all_gather(value if first is None else after(value, first), "leaf", axis=0)
        return [every[x] for x in range(need)]

    xa, xr, ys, factors = [], [], [], []
    early = 2 if small else 1
    cols = [over_leaf(picked[step], leaf_count) for step in range(early)]
    if small:
        own_col = over_leaf(picked[STEPS], leaf_count)
        root_own = root_pieces(after(high.astype(BF16), pieces[1]))
        root_all = after(root_all, row_map, place, own_col[-1], *[c[-1] for c in cols])
        roots = [root_pieces(root_all[0])]
    else:
        roots = [root_pieces(root_all[0])]
    done = [roots[0][-1]]
    for step in range(STEPS):
        if step and not small:
            cols.append(over_leaf(after(picked[step], done[-1]), leaf_count))
            roots.append(root_pieces(root_all[step], done[-1]))
        if step == 1 and not small:
            own_part = after(picked[STEPS], done[-1])
            own_col = over_leaf(own_part, leaf_count)
            root_own = root_pieces(high.astype(BF16), own_part)
        root_mine = root_all[step]
        root_step = roots[step]
        step_col = cols[step]
        last = step == STEPS - 1
        args = [*step_col, *root_step, root_mine]
        scratch = [
            pltpu.VMEM((slots, column.shape[0], PANEL), BF16),
            pltpu.VMEM((2, HALF, HALF), F32),
        ]
        if step:
            args += [*own_col, *root_own, *xa, *xr, *ys, mine, rest_block, *factors]
            scratch += [pltpu.VMEM((slots, device_rows, PANEL), BF16)]
        block = jax.ShapeDtypeStruct((device_rows, PANEL), F32)
        if last:
            shapes = [block]
            scratch += [
                pltpu.VMEM((5, HALF, HALF), F32),
                pltpu.VMEM((device_rows, PANEL), F32),
                pltpu.VMEM((device_rows, PANEL), BF16),
                pltpu.VMEM((PANEL, PANEL), BF16),
                pltpu.VMEM((device_rows, PANEL), F32),
                pltpu.VMEM((PANEL, PANEL), F32),
            ]
        else:
            scratch += [pltpu.VMEM(((STEPS - 1 - step) * PANEL, PANEL), F32)]
            shapes = [
                jax.ShapeDtypeStruct(((STEPS - 1 - step) * PANEL, PANEL), BF16),
                block,
                jax.ShapeDtypeStruct((5, HALF, HALF), F32),
            ]
            if step:
                shapes += [
                    jax.ShapeDtypeStruct((device_rows, PANEL), BF16),
                    jax.ShapeDtypeStruct((PANEL, PANEL), BF16),
                    block,
                ]
        out = pl.pallas_call(
            functools.partial(step_kernel, step, leaf_count, spots),
            in_specs=[SMEM_SPEC] + [VMEM_SPEC] * (1 + len(args)),
            out_specs=[VMEM_SPEC] * len(shapes),
            out_shape=shapes,
            scratch_shapes=scratch,
            compiler_params=params,
            cost_estimate=pl.CostEstimate(
                flops=15 * 10**9, transcendentals=0, bytes_accessed=4 * 2**20
            ),
        )(place, row_map, *[near(x) for x in args])
        if last:
            return out[0]
        xa.append(out[0])
        mine = out[1]
        factors.append(out[2])
        rest_block = root_entries
        if step:
            xr.append(out[3])
            ys.append(out[4])
            rest_block = out[5]
        done.append(out[0])
        if small and not last:
            if step + 2 < STEPS:
                cols.append(over_leaf(picked[step + 2], leaf_count, done[step], done[step + 1]))
            roots.append(root_pieces(root_all[step + 1], done[step], done[step + 1]))


def solution(mesh):
    spots = (P("leaf", "panel"), P("leaf", "panel"), P(), P())
    return jax.shard_map(
        per_device, mesh=mesh, in_specs=spots, out_specs=P("leaf", "panel"), check_vma=False
    )
```

```python
import functools

import jax
import jax.numpy as jnp
from jax import lax
from jax.experimental import pallas as pl
from jax.experimental.pallas import tpu as pltpu
from jax.sharding import PartitionSpec as P

PANEL = 256
STEPS = 5
HALF = PANEL // 2
SUB = 8
BAND = 32
DONE = STEPS * PANEL
HIGHEST = lax.Precision.HIGHEST
F32 = jnp.float32
BF16 = jnp.bfloat16
SMEM_SPEC = pl.BlockSpec(memory_space=pltpu.SMEM)
VMEM_SPEC = pl.BlockSpec(memory_space=pltpu.VMEM)


def mm(a, b, precision=None):
    return lax.dot_general(
        a, b, (((1,), (0,)), ((), ())), precision=precision, preferred_element_type=F32
    )


def mm_nt(a, b, precision=None):
    return lax.dot_general(
        a, b, (((1,), (1,)), ((), ())), precision=precision, preferred_element_type=F32
    )


def thirds(x):
    high = x.astype(BF16)
    rest = x - high.astype(F32)
    middle = rest.astype(BF16)
    return high, middle, (rest - middle.astype(F32)).astype(BF16)


def mm3_nt(a, b):
    ah, bh = a.astype(BF16), b.astype(BF16)
    al, bl = (a - ah.astype(F32)).astype(BF16), (b - bh.astype(F32)).astype(BF16)
    return mm_nt(jnp.concatenate([ah, ah, al], 1), jnp.concatenate([bh, bl, bh], 1))


def mm3(a, b):
    ah, bh = a.astype(BF16), b.astype(BF16)
    al, bl = (a - ah.astype(F32)).astype(BF16), (b - bh.astype(F32)).astype(BF16)
    return mm(jnp.concatenate([ah, ah, al], 1), jnp.concatenate([bh, bl, bh], 0))


def factor_half(a):
    n = a.shape[0]
    groups = BAND // SUB
    lane = lax.broadcasted_iota(jnp.int32, (SUB, n), 1)
    sub = lax.broadcasted_iota(jnp.int32, (SUB, n), 0)
    band_lane = lax.broadcasted_iota(jnp.int32, (BAND, n), 1)
    band_sub = lax.broadcasted_iota(jnp.int32, (BAND, n), 0)

    def full(v):
        return jnp.broadcast_to(v, (SUB, n))

    left = a
    uppers, inverses = [], []
    for base in range(0, n, BAND):
        rows = [left[SUB * g : SUB * g + SUB, :] for g in range(groups)]
        inv = [
            jnp.where(lane < base, rows[g], jnp.where(lane == sub + (base + SUB * g), 1.0, 0.0))
            for g in range(groups)
        ]
        for g in range(groups):
            below = groups - g
            at = base + SUB * g
            col = [
                [full(rows[g + h][:, at + q : at + q + 1]) for h in range(below)] for q in range(SUB)
            ]
            tip = [
                [full(col[q][0][r : r + 1, :]) if r >= q else None for r in range(SUB)]
                for q in range(SUB)
            ]
            for q in range(SUB):
                scale = lax.rsqrt(tip[q][q])
                part = [tip[q][r] * scale if r > q else None for r in range(SUB)]
                for q2 in range(q + 1, SUB):
                    for r in range(q2, SUB):
                        tip[q2][r] = tip[q2][r] - part[r] * part[q2]
                mult = [col[q][h] * scale for h in range(below)]
                mult[0] = jnp.where(sub > q, mult[0], 0.0)
                for q2 in range(q + 1, SUB):
                    for h in range(below):
                        col[q2][h] = col[q2][h] - mult[h] * part[q2]
                for x in (rows, inv):
                    row = full(x[g][q : q + 1, :]) * scale
                    x[g] = jnp.where(sub == q, row, x[g] - mult[0] * row)
                    for h in range(1, below):
                        x[g + h] = x[g + h] - mult[h] * row
        upper = jnp.concatenate(rows, 0)
        inverse = jnp.concatenate(inv, 0)
        uppers.append(jnp.where(band_lane >= band_sub + base, upper, 0.0))
        inverses.append(inverse)
        if base + BAND < n:
            both = jnp.where(band_lane < base + BAND, inverse, upper)
            uh, um, ul = thirds(upper)
            bh, bm, bl = thirds(both)
            product = lax.dot_general(
                jnp.concatenate([uh, uh, um, uh, ul, um], 0),
                jnp.concatenate([bh, bm, bh, bl, bh, bm], 0),
                (((0,), (0,)), ((), ())),
                preferred_element_type=F32,
            )
            left = left[BAND:, :]
            at = lax.broadcasted_iota(jnp.int32, left.shape, 1)
            left = jnp.where((at >= base) & (at < base + BAND), 0.0, left) - product[base + BAND :, :]
    return jnp.concatenate(uppers, 0), jnp.concatenate(inverses, 0)


def select_kernel(bases_ref, keep_ref, map_ref, *refs):
    count = bases_ref.shape[0]
    pieces, outs = refs[:-count], refs[-count:]
    width = pieces[0].shape[1]
    tiles = keep_ref.shape[0]
    tile = pieces[0].shape[0] // tiles
    kept = []
    for k, piece in enumerate(pieces):
        kept.append(
            jnp.concatenate(
                [
                    piece[t * tile : (t + 1) * tile, :] * keep_ref[t, k].astype(F32).astype(BF16)
                    for t in range(tiles)
                ],
                0,
            )
        )
    kept = jnp.concatenate(kept, 1)
    ids = lax.broadcasted_iota(jnp.int32, (PANEL, 1), 0)
    for block in range(count):
        hot = (ids + bases_ref[block] == map_ref[...]).astype(F32).astype(BF16)
        outs[block][...] = mm_nt(kept, hot).astype(BF16)


def placed(row_base, count, map_ref, pieces, lanes=slice(None)):
    width = pieces[0].shape[0]
    ids = lax.broadcasted_iota(jnp.int32, (count, 1), 0) + row_base
    total = None
    for x, piece in enumerate(pieces):
        hot = (ids == map_ref[:, x * width : (x + 1) * width]).astype(F32).astype(BF16)
        term = mm(hot, piece[:, lanes])
        total = term if total is None else total + term
    return total


def solve_right(g, i1, l21, i2):
    one = mm3_nt(g[:, :HALF], i1)
    two = mm3_nt(g[:, HALF:] - mm3_nt(one, l21), i2)
    return jnp.concatenate([one, two], 1)


def solve_left(h, i1, l21, i2):
    one = mm3(i1, h[:HALF, :])
    two = mm3(i2, h[HALF:, :] - mm3(l21, one))
    return jnp.concatenate([one, two], 0)


def step_kernel(step, leaves, spots, *refs):
    refs = list(refs)

    def take(count):
        out = refs[:count]
        del refs[:count]
        return out

    (place_ref, map_ref) = take(2)
    step_col, root_step, (root_mine,) = take(leaves), take(spots), take(1)
    prev = step - 1
    last = step == STEPS - 1
    if step:
        own_col, root_own = take(leaves), take(spots)
        before_a, before_r, before_y = take(step), take(prev), take(prev)
        (sum_ref, rest_ref) = take(2)
        factors = take(step)
    if last:
        (out_ref,) = take(1)
        (fac_ref, gr_ref, xr_ref, y_ref, t_ref, h_ref) = refs[-6:]
    else:
        (xa_ref, gr_ref, fac_ref) = take(3)
        if step:
            (xr_ref, y_ref, t_ref) = take(3)
    (root_s, d_s) = take(2)
    if step:
        (rown_s,) = take(1)
    if not last:
        (g_s,) = take(1)
    device_rows = step_col[0].shape[0]
    per_leaf = device_rows // PANEL
    panel = place_ref[1]
    base = place_ref[0] * device_rows
    for x in range(spots):
        leaf = place_ref[2 + x]
        root_s[leaf] = root_step[x][...]
        if step:
            rown_s[leaf] = root_own[x][...]

    def panel_rows(m, r):
        return before_a[m][(r - m - 1) * PANEL : (r - m) * PANEL, :]

    def own_rows(r, lanes):
        return rown_s[r // per_leaf, pl.ds(r % per_leaf * PANEL, PANEL), lanes].astype(F32)

    share = root_s.shape[1] - device_rows
    if share == PANEL:
        rest = root_s[step // per_leaf, pl.ds(device_rows, PANEL), :]
    else:
        rest = jnp.concatenate(
            [root_s[x, pl.ds(device_rows, share), :] for x in range(PANEL // share)], 0
        )
    diag = root_s[step // per_leaf, pl.ds(step % per_leaf * PANEL, PANEL), :].astype(F32)
    diag = diag + rest.astype(F32) + placed(step * PANEL, PANEL, map_ref, step_col)
    for m in range(step):
        diag = diag - mm_nt(panel_rows(m, step), panel_rows(m, step))
    d_s[0] = diag[:HALF, :HALF]
    d_s[1] = diag[HALF:, HALF:]
    fac_ref[1] = diag[HALF:, :HALF]
    pieces = STEPS - 1 - step
    part = device_rows // 2

    def half(n, carry):
        upper, inverse = factor_half(d_s[n])
        fac_ref[2 * n] = upper
        fac_ref[3 + n] = inverse
        if not last:
            count = pieces * HALF
            here = pl.ds(pl.multiple_of(n * count, HALF), count)
            start = (step + 1) * PANEL + n * count
            found = []
            for c in range(pieces):
                row = start + c * HALF
                at = pl.ds(pl.multiple_of(row % device_rows, HALF), HALF)
                found.append(root_s[row // device_rows, at, :])
            g = jnp.concatenate(found, 0).astype(F32) + placed(start, count, map_ref, step_col)
            for m in range(step):
                at = pl.ds(pl.multiple_of((step - m) * PANEL + n * count, HALF), count)
                g = g - mm_nt(before_a[m][at, :], panel_rows(m, step))
            g_s[here, :] = g
        rows = pl.ds(pl.multiple_of(n * part, HALF), part)
        mine = root_mine[rows, :].astype(F32) + placed(base + n * part, part, map_ref, step_col)
        if step:
            fac = factors[prev]
            p1, pl21, p2 = fac[3], fac[1], fac[4]
            xr = solve_right(sum_ref[rows, :], p1, pl21, p2).astype(BF16)
            for m in range(prev):
                mine = mine - mm_nt(before_r[m][rows, :], panel_rows(m, step))
            mine = mine - mm_nt(xr, panel_rows(prev, step))
            xr_ref[rows, :] = xr
            lanes = pl.ds(pl.multiple_of(n * HALF, HALF), HALF)
            h = own_rows(prev, lanes) + placed(prev * PANEL, PANEL, map_ref, own_col, lanes)
            for m in range(prev):
                h = h - mm(panel_rows(m, prev), before_y[m][:, lanes])
            y = solve_left(h, p1, pl21, p2).astype(BF16)
            y_ref[:, lanes] = y
            t = rest_ref[rows, :]
            if step == 1:
                t = t + placed(base + n * part, part, map_ref, own_col)
            else:
                use = jnp.where(step - 2 < panel, 1.0, 0.0).astype(BF16)
                t = t - mm(before_r[step - 2][rows, :], before_y[step - 2][...] * use)
            t_ref[rows, :] = t
            if last:
                h = own_rows(step, lanes) + placed(step * PANEL, PANEL, map_ref, own_col, lanes)
                for m in range(prev):
                    h = h - mm(panel_rows(m, step), before_y[m][:, lanes])
                h_ref[:, lanes] = h - mm(panel_rows(prev, step), y)
        gr_ref[rows, :] = mine

        @pl.when(n == 0)
        def _():
            low = mm3_nt(fac_ref[1], inverse)
            fac_ref[1] = low
            d_s[1] = d_s[1] - mm3_nt(low, low)

        return carry

    lax.fori_loop(0, 2, half, 0)
    l21, i1, i2 = fac_ref[1], fac_ref[3], fac_ref[4]
    if not last:
        xa_ref[...] = solve_right(g_s[...], i1, l21, i2).astype(BF16)
        return
    rows = lax.broadcasted_iota(jnp.int32, (device_rows, 1), 0) + base
    use = jnp.where(prev < panel, 1.0, 0.0).astype(BF16)
    t = t_ref[...] - mm(xr_ref[...], y_ref[...] * use)

    @pl.when(panel >= STEPS)
    def _():
        xr = solve_right(gr_ref[...], i1, l21, i2).astype(BF16)
        y = solve_left(h_ref[...], i1, l21, i2).astype(BF16)
        out_ref[...] = jnp.where(rows >= DONE, t - mm(xr, y), 0.0)

    for m in range(STEPS - 1):

        @pl.when(panel == m)
        def _():
            fac_ref[...] = factors[m][...]

    @pl.when(panel < STEPS)
    def _():
        solved = solve_right(t, fac_ref[3], fac_ref[1], fac_ref[4])
        out_ref[...] = jnp.where(rows >= (panel + 1) * PANEL, solved, 0.0)
        for part in range(device_rows // PANEL):
            start = part * PANEL

            @pl.when(base + start == panel * PANEL)
            def _():
                out_ref[start : start + HALF, :HALF] = fac_ref[0].T
                out_ref[start + HALF : start + PANEL, :HALF] = fac_ref[1]
                out_ref[start + HALF : start + PANEL, HALF:] = fac_ref[2].T


def flip(value, axis, bits, count):
    return lax.ppermute(value, axis, [(i, i ^ bits) for i in range(count)])


def after(value, *held):
    return lax.optimization_barrier((value, *held))[0]


def over_leaf(value, leaf_count, first=None, second=None):
    if first is not None:
        value = after(value, first)
    parts = {0: value}
    bit = leaf_count // 2
    while bit:
        for have in list(parts):
            part = parts[have] if second is None or not have else after(parts[have], second)
            parts[have | bit] = flip(part, "leaf", bit, leaf_count)
        bit //= 2
    return [parts[x] for x in range(leaf_count)]


def over_panel(value, panel_count):
    parts = {0: value}
    bit = panel_count // 2
    while bit > 2:
        for have in list(parts):
            parts[have | bit] = flip(parts[have], "panel", bit, panel_count)
        bit //= 2
    for have in list(parts):
        for near in range(1, 2 * bit):
            parts[have | near] = flip(parts[have], "panel", near, panel_count)
    return [parts[x] for x in range(panel_count)]


def per_device(root_entries, child_updates, child_map, tile_pattern):
    device_rows, panel_width = root_entries.shape
    child_cols = child_updates.shape[1]
    leaf_count = lax.axis_size("leaf")
    panel_count = lax.axis_size("panel")
    leaf = lax.axis_index("leaf")
    panel = lax.axis_index("panel")
    child_order = child_cols * panel_count
    half_leaf = leaf_count // 2
    tile_width = child_order // tile_pattern.shape[1]
    tiles = device_rows // tile_width
    child = leaf // half_leaf
    small = leaf_count == 4 and panel_count == 8
    params = pltpu.CompilerParams(vmem_limit_bytes=(20 if small else 56) * 2**20)

    def near(x):
        return pltpu.with_memory_space_constraint(x, pltpu.VMEM) if small else x

    high = lax.reduce_precision(root_entries, 8, 7)
    offset = panel * PANEL % device_rows
    rest = lax.dynamic_slice_in_dim(root_entries - high, offset, PANEL, 0)
    rest = rest.astype(BF16)
    if small:
        share = PANEL // leaf_count
        holder = jnp.minimum(panel * PANEL // device_rows, leaf_count - 1)
        shares = [
            lax.dynamic_slice_in_dim(rest, (leaf ^ x) * share, share, 0) for x in range(leaf_count)
        ]
        shares = shares[:1] + [flip(shares[x], "leaf", x, leaf_count) for x in range(1, leaf_count)]
        rest = shares[0]
        for x in range(1, leaf_count):
            rest = jnp.where(leaf ^ x == holder, shares[x], rest)
    column = jnp.concatenate([high.astype(BF16), rest], 0)

    pieces = over_panel(child_updates, panel_count)
    if small:
        columns = over_panel(column, panel_count)
        root_all = jnp.zeros((STEPS + 1, *column.shape), BF16)
        for x in (0, 4, 1, 2, 3, 5, 6, 7):
            slot = jnp.minimum(panel ^ x, STEPS)
            root_all = lax.dynamic_update_slice(root_all, columns[x][None], (slot, 0, 0))
    else:
        root_all = lax.all_gather(column, "panel", axis=0)
    order = panel ^ jnp.arange(panel_count, dtype=jnp.int32)
    own_map = lax.dynamic_index_in_dim(child_map, child, 0, keepdims=False)
    col_map = own_map.reshape(panel_count, child_cols)[order].reshape(1, child_order)
    pattern = lax.dynamic_index_in_dim(tile_pattern, child, 0, keepdims=False)
    mirrored = jnp.maximum(pattern, pattern.T)
    keep = lax.dynamic_slice_in_dim(mirrored, leaf % half_leaf * tiles, tiles, 0)[:, order]
    keep = (keep > 0).astype(jnp.int32)

    def select(bases):
        count = bases.shape[0]
        return pl.pallas_call(
            select_kernel,
            in_specs=[SMEM_SPEC, SMEM_SPEC, VMEM_SPEC] + [VMEM_SPEC] * panel_count,
            out_specs=[VMEM_SPEC] * count,
            out_shape=[jax.ShapeDtypeStruct((device_rows, PANEL), BF16)] * count,
            compiler_params=params,
            cost_estimate=pl.CostEstimate(
                flops=10**9 * count, transcendentals=0, bytes_accessed=2**20
            ),
        )(bases, keep, col_map, *pieces)

    starts = jnp.arange(STEPS, dtype=jnp.int32) * PANEL
    picked = select(starts[:1])
    picked += select(jnp.concatenate([starts[1:], (panel * PANEL)[None].astype(jnp.int32)]))

    leaf_order = leaf ^ jnp.arange(leaf_count, dtype=jnp.int32)
    row_map = child_map.reshape(leaf_count, device_rows)[leaf_order].reshape(1, 2 * child_order)
    need = -(-DONE // device_rows)
    spots = leaf_count if small else need
    slots = max(spots, need)
    spot_order = leaf_order if small else jnp.arange(need, dtype=jnp.int32)
    place = jnp.concatenate([jnp.stack([leaf, panel]).astype(jnp.int32), spot_order])

    def root_pieces(value, first=None, second=None):
        if small:
            return over_leaf(value, leaf_count, first, second)
        every = lax.all_gather(value if first is None else after(value, first), "leaf", axis=0)
        return [every[x] for x in range(need)]

    xa, xr, ys, factors = [], [], [], []
    early = 3 if small else 1
    if small:
        root_own = root_pieces(after(high.astype(BF16), pieces[1]))
        picked = [after(picked[0], root_own[-1]), *picked[1:]]
    cols = [over_leaf(picked[step], leaf_count) for step in range(early)]
    if small:
        own_col = over_leaf(picked[STEPS], leaf_count)
        root_all = after(root_all, row_map, place, own_col[-1], cols[0][-1], cols[1][-1])
        roots = [root_pieces(root_all[0])]
    else:
        roots = [root_pieces(root_all[0])]
    done = [roots[0][-1]]
    for step in range(STEPS):
        if step and not small:
            cols.append(over_leaf(after(picked[step], done[-1]), leaf_count))
            roots.append(root_pieces(root_all[step], done[-1]))
        if step == 1 and not small:
            own_part = after(picked[STEPS], done[-1])
            own_col = over_leaf(own_part, leaf_count)
            root_own = root_pieces(high.astype(BF16), own_part)
        root_mine = root_all[step]
        root_step = roots[step]
        step_col = cols[step]
        last = step == STEPS - 1
        args = [*step_col, *root_step, root_mine]
        scratch = [
            pltpu.VMEM((slots, column.shape[0], PANEL), BF16),
            pltpu.VMEM((2, HALF, HALF), F32),
        ]
        if step:
            args += [*own_col, *root_own, *xa, *xr, *ys, mine, rest_block, *factors]
            scratch += [pltpu.VMEM((slots, device_rows, PANEL), BF16)]
        block = jax.ShapeDtypeStruct((device_rows, PANEL), F32)
        if last:
            shapes = [block]
            scratch += [
                pltpu.VMEM((5, HALF, HALF), F32),
                pltpu.VMEM((device_rows, PANEL), F32),
                pltpu.VMEM((device_rows, PANEL), BF16),
                pltpu.VMEM((PANEL, PANEL), BF16),
                pltpu.VMEM((device_rows, PANEL), F32),
                pltpu.VMEM((PANEL, PANEL), F32),
            ]
        else:
            scratch += [pltpu.VMEM(((STEPS - 1 - step) * PANEL, PANEL), F32)]
            shapes = [
                jax.ShapeDtypeStruct(((STEPS - 1 - step) * PANEL, PANEL), BF16),
                block,
                jax.ShapeDtypeStruct((5, HALF, HALF), F32),
            ]
            if step:
                shapes += [
                    jax.ShapeDtypeStruct((device_rows, PANEL), BF16),
                    jax.ShapeDtypeStruct((PANEL, PANEL), BF16),
                    block,
                ]
        out = pl.pallas_call(
            functools.partial(step_kernel, step, leaf_count, spots),
            in_specs=[SMEM_SPEC] + [VMEM_SPEC] * (1 + len(args)),
            out_specs=[VMEM_SPEC] * len(shapes),
            out_shape=shapes,
            scratch_shapes=scratch,
            compiler_params=params,
            cost_estimate=pl.CostEstimate(
                flops=15 * 10**9, transcendentals=0, bytes_accessed=4 * 2**20
            ),
        )(place, row_map, *[near(x) for x in args])
        if last:
            return out[0]
        xa.append(out[0])
        mine = out[1]
        factors.append(out[2])
        rest_block = root_entries
        if step:
            xr.append(out[3])
            ys.append(out[4])
            rest_block = out[5]
        done.append(out[0])
        if small and not last:
            roots.append(root_pieces(root_all[step + 1], done[step], done[step + 1]))
            if step and step + 2 < STEPS:
                cols.append(over_leaf(picked[step + 2], leaf_count, done[step], done[step + 1]))


def solution(mesh):
    spots = (P("leaf", "panel"), P("leaf", "panel"), P(), P())
    return jax.shard_map(
        per_device, mesh=mesh, in_specs=spots, out_specs=P("leaf", "panel"), check_vma=False
    )
```

```python
import functools

import jax
import jax.numpy as jnp
from jax import lax
from jax.experimental import pallas as pl
from jax.experimental.pallas import tpu as pltpu
from jax.sharding import PartitionSpec as P

PANEL = 256
STEPS = 5
HALF = PANEL // 2
SUB = 8
BAND = 32
DONE = STEPS * PANEL
HIGHEST = lax.Precision.HIGHEST
F32 = jnp.float32
BF16 = jnp.bfloat16
SMEM_SPEC = pl.BlockSpec(memory_space=pltpu.SMEM)
VMEM_SPEC = pl.BlockSpec(memory_space=pltpu.VMEM)


def mm(a, b, precision=None):
    return lax.dot_general(
        a, b, (((1,), (0,)), ((), ())), precision=precision, preferred_element_type=F32
    )


def mm_nt(a, b, precision=None):
    return lax.dot_general(
        a, b, (((1,), (1,)), ((), ())), precision=precision, preferred_element_type=F32
    )


def thirds(x):
    high = x.astype(BF16)
    rest = x - high.astype(F32)
    middle = rest.astype(BF16)
    return high, middle, (rest - middle.astype(F32)).astype(BF16)


def mm3_nt(a, b):
    ah, bh = a.astype(BF16), b.astype(BF16)
    al, bl = (a - ah.astype(F32)).astype(BF16), (b - bh.astype(F32)).astype(BF16)
    return mm_nt(jnp.concatenate([ah, ah, al], 1), jnp.concatenate([bh, bl, bh], 1))


def mm3(a, b):
    ah, bh = a.astype(BF16), b.astype(BF16)
    al, bl = (a - ah.astype(F32)).astype(BF16), (b - bh.astype(F32)).astype(BF16)
    return mm(jnp.concatenate([ah, ah, al], 1), jnp.concatenate([bh, bl, bh], 0))


def factor_half(a):
    n = a.shape[0]
    groups = BAND // SUB
    lane = lax.broadcasted_iota(jnp.int32, (SUB, n), 1)
    sub = lax.broadcasted_iota(jnp.int32, (SUB, n), 0)
    band_lane = lax.broadcasted_iota(jnp.int32, (BAND, n), 1)
    band_sub = lax.broadcasted_iota(jnp.int32, (BAND, n), 0)

    def full(v):
        return jnp.broadcast_to(v, (SUB, n))

    left = a
    uppers, inverses = [], []
    for base in range(0, n, BAND):
        rows = [left[SUB * g : SUB * g + SUB, :] for g in range(groups)]
        inv = [
            jnp.where(lane < base, rows[g], jnp.where(lane == sub + (base + SUB * g), 1.0, 0.0))
            for g in range(groups)
        ]
        for g in range(groups):
            below = groups - g
            at = base + SUB * g
            col = [
                [full(rows[g + h][:, at + q : at + q + 1]) for h in range(below)] for q in range(SUB)
            ]
            tip = [
                [full(col[q][0][r : r + 1, :]) if r >= q else None for r in range(SUB)]
                for q in range(SUB)
            ]
            for q in range(SUB):
                scale = lax.rsqrt(tip[q][q])
                part = [tip[q][r] * scale if r > q else None for r in range(SUB)]
                for q2 in range(q + 1, SUB):
                    for r in range(q2, SUB):
                        tip[q2][r] = tip[q2][r] - part[r] * part[q2]
                mult = [col[q][h] * scale for h in range(below)]
                mult[0] = jnp.where(sub > q, mult[0], 0.0)
                for q2 in range(q + 1, SUB):
                    for h in range(below):
                        col[q2][h] = col[q2][h] - mult[h] * part[q2]
                for x in (rows, inv):
                    row = full(x[g][q : q + 1, :]) * scale
                    x[g] = jnp.where(sub == q, row, x[g] - mult[0] * row)
                    for h in range(1, below):
                        x[g + h] = x[g + h] - mult[h] * row
        upper = jnp.concatenate(rows, 0)
        inverse = jnp.concatenate(inv, 0)
        uppers.append(jnp.where(band_lane >= band_sub + base, upper, 0.0))
        inverses.append(inverse)
        if base + BAND < n:
            both = jnp.where(band_lane < base + BAND, inverse, upper)
            uh, um, ul = thirds(upper)
            bh, bm, bl = thirds(both)
            product = lax.dot_general(
                jnp.concatenate([uh, uh, um, uh, ul, um], 0),
                jnp.concatenate([bh, bm, bh, bl, bh, bm], 0),
                (((0,), (0,)), ((), ())),
                preferred_element_type=F32,
            )
            left = left[BAND:, :]
            at = lax.broadcasted_iota(jnp.int32, left.shape, 1)
            left = jnp.where((at >= base) & (at < base + BAND), 0.0, left) - product[base + BAND :, :]
    return jnp.concatenate(uppers, 0), jnp.concatenate(inverses, 0)


def select_kernel(bases_ref, keep_ref, map_ref, *refs):
    count = bases_ref.shape[0]
    pieces, outs = refs[:-count], refs[-count:]
    width = pieces[0].shape[1]
    tiles = keep_ref.shape[0]
    tile = pieces[0].shape[0] // tiles
    kept = []
    for k, piece in enumerate(pieces):
        kept.append(
            jnp.concatenate(
                [
                    piece[t * tile : (t + 1) * tile, :] * keep_ref[t, k].astype(F32).astype(BF16)
                    for t in range(tiles)
                ],
                0,
            )
        )
    kept = jnp.concatenate(kept, 1)
    ids = lax.broadcasted_iota(jnp.int32, (PANEL, 1), 0)
    for block in range(count):
        hot = (ids + bases_ref[block] == map_ref[...]).astype(F32).astype(BF16)
        outs[block][...] = mm_nt(kept, hot).astype(BF16)


def placed(row_base, count, map_ref, pieces, lanes=slice(None)):
    width = pieces[0].shape[0]
    ids = lax.broadcasted_iota(jnp.int32, (count, 1), 0) + row_base
    total = None
    for x, piece in enumerate(pieces):
        hot = (ids == map_ref[:, x * width : (x + 1) * width]).astype(F32).astype(BF16)
        term = mm(hot, piece[:, lanes])
        total = term if total is None else total + term
    return total


def solve_right(g, i1, l21, i2):
    one = mm3_nt(g[:, :HALF], i1)
    two = mm3_nt(g[:, HALF:] - mm3_nt(one, l21), i2)
    return jnp.concatenate([one, two], 1)


def solve_left(h, i1, l21, i2):
    one = mm3(i1, h[:HALF, :])
    two = mm3(i2, h[HALF:, :] - mm3(l21, one))
    return jnp.concatenate([one, two], 0)


def step_kernel(step, leaves, spots, *refs):
    refs = list(refs)

    def take(count):
        out = refs[:count]
        del refs[:count]
        return out

    (place_ref, map_ref) = take(2)
    step_col, root_step, (root_mine,) = take(leaves), take(spots), take(1)
    prev = step - 1
    last = step == STEPS - 1
    if step:
        own_col, root_own = take(leaves), take(spots)
        before_a, before_r, before_y = take(step), take(prev), take(prev)
        (sum_ref, rest_ref) = take(2)
        factors = take(step)
    if last:
        (out_ref,) = take(1)
        (fac_ref, gr_ref, xr_ref, y_ref, t_ref, h_ref) = refs[-6:]
    else:
        (xa_ref, gr_ref, fac_ref) = take(3)
        if step:
            (xr_ref, y_ref, t_ref) = take(3)
    (root_s, d_s) = take(2)
    if step:
        (rown_s,) = take(1)
    if not last:
        (g_s,) = take(1)
    device_rows = step_col[0].shape[0]
    per_leaf = device_rows // PANEL
    panel = place_ref[1]
    base = place_ref[0] * device_rows
    for x in range(spots):
        leaf = place_ref[2 + x]
        root_s[leaf] = root_step[x][...]
        if step:
            rown_s[leaf] = root_own[x][...]

    def panel_rows(m, r):
        return before_a[m][(r - m - 1) * PANEL : (r - m) * PANEL, :]

    def own_rows(r, lanes):
        return rown_s[r // per_leaf, pl.ds(r % per_leaf * PANEL, PANEL), lanes].astype(F32)

    share = root_s.shape[1] - device_rows
    if share == PANEL:
        rest = root_s[step // per_leaf, pl.ds(device_rows, PANEL), :]
    else:
        rest = jnp.concatenate(
            [root_s[x, pl.ds(device_rows, share), :] for x in range(PANEL // share)], 0
        )
    diag = root_s[step // per_leaf, pl.ds(step % per_leaf * PANEL, PANEL), :].astype(F32)
    diag = diag + rest.astype(F32) + placed(step * PANEL, PANEL, map_ref, step_col)
    for m in range(step):
        diag = diag - mm_nt(panel_rows(m, step), panel_rows(m, step))
    d_s[0] = diag[:HALF, :HALF]
    d_s[1] = diag[HALF:, HALF:]
    fac_ref[1] = diag[HALF:, :HALF]
    pieces = STEPS - 1 - step
    part = device_rows // 2

    def half(n, carry):
        upper, inverse = factor_half(d_s[n])
        fac_ref[2 * n] = upper
        fac_ref[3 + n] = inverse
        if not last:
            count = pieces * HALF
            here = pl.ds(pl.multiple_of(n * count, HALF), count)
            start = (step + 1) * PANEL + n * count
            found = []
            for c in range(pieces):
                row = start + c * HALF
                at = pl.ds(pl.multiple_of(row % device_rows, HALF), HALF)
                found.append(root_s[row // device_rows, at, :])
            g = jnp.concatenate(found, 0).astype(F32) + placed(start, count, map_ref, step_col)
            for m in range(step):
                at = pl.ds(pl.multiple_of((step - m) * PANEL + n * count, HALF), count)
                g = g - mm_nt(before_a[m][at, :], panel_rows(m, step))
            g_s[here, :] = g
        rows = pl.ds(pl.multiple_of(n * part, HALF), part)
        mine = root_mine[rows, :].astype(F32) + placed(base + n * part, part, map_ref, step_col)
        if step:
            fac = factors[prev]
            p1, pl21, p2 = fac[3], fac[1], fac[4]
            xr = solve_right(sum_ref[rows, :], p1, pl21, p2).astype(BF16)
            for m in range(prev):
                mine = mine - mm_nt(before_r[m][rows, :], panel_rows(m, step))
            mine = mine - mm_nt(xr, panel_rows(prev, step))
            xr_ref[rows, :] = xr
            lanes = pl.ds(pl.multiple_of(n * HALF, HALF), HALF)
            h = own_rows(prev, lanes) + placed(prev * PANEL, PANEL, map_ref, own_col, lanes)
            for m in range(prev):
                h = h - mm(panel_rows(m, prev), before_y[m][:, lanes])
            y = solve_left(h, p1, pl21, p2).astype(BF16)
            y_ref[:, lanes] = y
            t = rest_ref[rows, :]
            if step == 1:
                t = t + placed(base + n * part, part, map_ref, own_col)
            else:
                use = jnp.where(step - 2 < panel, 1.0, 0.0).astype(BF16)
                t = t - mm(before_r[step - 2][rows, :], before_y[step - 2][...] * use)
            t_ref[rows, :] = t
            if last:
                h = own_rows(step, lanes) + placed(step * PANEL, PANEL, map_ref, own_col, lanes)
                for m in range(prev):
                    h = h - mm(panel_rows(m, step), before_y[m][:, lanes])
                h_ref[:, lanes] = h - mm(panel_rows(prev, step), y)
        gr_ref[rows, :] = mine

        @pl.when(n == 0)
        def _():
            low = mm3_nt(fac_ref[1], inverse)
            fac_ref[1] = low
            d_s[1] = d_s[1] - mm3_nt(low, low)

        return carry

    lax.fori_loop(0, 2, half, 0)
    l21, i1, i2 = fac_ref[1], fac_ref[3], fac_ref[4]
    if not last:
        xa_ref[...] = solve_right(g_s[...], i1, l21, i2).astype(BF16)
        return
    rows = lax.broadcasted_iota(jnp.int32, (device_rows, 1), 0) + base
    use = jnp.where(prev < panel, 1.0, 0.0).astype(BF16)
    t = t_ref[...] - mm(xr_ref[...], y_ref[...] * use)

    @pl.when(panel >= STEPS)
    def _():
        xr = solve_right(gr_ref[...], i1, l21, i2).astype(BF16)
        y = solve_left(h_ref[...], i1, l21, i2).astype(BF16)
        out_ref[...] = jnp.where(rows >= DONE, t - mm(xr, y), 0.0)

    for m in range(STEPS - 1):

        @pl.when(panel == m)
        def _():
            fac_ref[...] = factors[m][...]

    @pl.when(panel < STEPS)
    def _():
        solved = solve_right(t, fac_ref[3], fac_ref[1], fac_ref[4])
        out_ref[...] = jnp.where(rows >= (panel + 1) * PANEL, solved, 0.0)
        for part in range(device_rows // PANEL):
            start = part * PANEL

            @pl.when(base + start == panel * PANEL)
            def _():
                out_ref[start : start + HALF, :HALF] = fac_ref[0].T
                out_ref[start + HALF : start + PANEL, :HALF] = fac_ref[1]
                out_ref[start + HALF : start + PANEL, HALF:] = fac_ref[2].T


def flip(value, axis, bits, count):
    return lax.ppermute(value, axis, [(i, i ^ bits) for i in range(count)])


def after(value, *held):
    return lax.optimization_barrier((value, *held))[0]


def over_leaf(value, leaf_count, first=None, second=None):
    if first is not None:
        value = after(value, first)
    parts = {0: value}
    bit = leaf_count // 2
    while bit:
        for have in list(parts):
            part = parts[have] if second is None or not have else after(parts[have], second)
            parts[have | bit] = flip(part, "leaf", bit, leaf_count)
        bit //= 2
    return [parts[x] for x in range(leaf_count)]


def over_panel(value, panel_count):
    parts = {0: value}
    bit = panel_count // 2
    while bit > 2:
        for have in list(parts):
            parts[have | bit] = flip(parts[have], "panel", bit, panel_count)
        bit //= 2
    for have in list(parts):
        for near in range(1, 2 * bit):
            parts[have | near] = flip(parts[have], "panel", near, panel_count)
    return [parts[x] for x in range(panel_count)]


def per_device(root_entries, child_updates, child_map, tile_pattern):
    device_rows, panel_width = root_entries.shape
    child_cols = child_updates.shape[1]
    leaf_count = lax.axis_size("leaf")
    panel_count = lax.axis_size("panel")
    leaf = lax.axis_index("leaf")
    panel = lax.axis_index("panel")
    child_order = child_cols * panel_count
    half_leaf = leaf_count // 2
    tile_width = child_order // tile_pattern.shape[1]
    tiles = device_rows // tile_width
    child = leaf // half_leaf
    small = leaf_count == 4 and panel_count == 8
    params = pltpu.CompilerParams(vmem_limit_bytes=(20 if small else 56) * 2**20)

    def near(x):
        return pltpu.with_memory_space_constraint(x, pltpu.VMEM) if small else x

    high = lax.reduce_precision(root_entries, 8, 7)
    offset = panel * PANEL % device_rows
    rest = lax.dynamic_slice_in_dim(root_entries - high, offset, PANEL, 0)
    rest = rest.astype(BF16)
    if small:
        share = PANEL // leaf_count
        holder = jnp.minimum(panel * PANEL // device_rows, leaf_count - 1)
        shares = [
            lax.dynamic_slice_in_dim(rest, (leaf ^ x) * share, share, 0) for x in range(leaf_count)
        ]
        shares = shares[:1] + [flip(shares[x], "leaf", x, leaf_count) for x in range(1, leaf_count)]
        rest = shares[0]
        for x in range(1, leaf_count):
            rest = jnp.where(leaf ^ x == holder, shares[x], rest)
    column = jnp.concatenate([high.astype(BF16), rest], 0)

    pieces = over_panel(child_updates, panel_count)
    if small:
        columns = over_panel(column, panel_count)
        root_all = jnp.zeros((STEPS + 1, *column.shape), BF16)
        for x in (0, 4, 1, 2, 3, 5, 6, 7):
            slot = jnp.minimum(panel ^ x, STEPS)
            root_all = lax.dynamic_update_slice(root_all, columns[x][None], (slot, 0, 0))
    else:
        root_all = lax.all_gather(column, "panel", axis=0)
    order = panel ^ jnp.arange(panel_count, dtype=jnp.int32)
    own_map = lax.dynamic_index_in_dim(child_map, child, 0, keepdims=False)
    col_map = own_map.reshape(panel_count, child_cols)[order].reshape(1, child_order)
    pattern = lax.dynamic_index_in_dim(tile_pattern, child, 0, keepdims=False)
    mirrored = jnp.maximum(pattern, pattern.T)
    keep = lax.dynamic_slice_in_dim(mirrored, leaf % half_leaf * tiles, tiles, 0)[:, order]
    keep = (keep > 0).astype(jnp.int32)

    def select(bases):
        count = bases.shape[0]
        return pl.pallas_call(
            select_kernel,
            in_specs=[SMEM_SPEC, SMEM_SPEC, VMEM_SPEC] + [VMEM_SPEC] * panel_count,
            out_specs=[VMEM_SPEC] * count,
            out_shape=[jax.ShapeDtypeStruct((device_rows, PANEL), BF16)] * count,
            compiler_params=params,
            cost_estimate=pl.CostEstimate(
                flops=10**9 * count, transcendentals=0, bytes_accessed=2**20
            ),
        )(bases, keep, col_map, *pieces)

    starts = jnp.arange(STEPS, dtype=jnp.int32) * PANEL
    picked = select(jnp.concatenate([starts, (panel * PANEL)[None].astype(jnp.int32)]))

    leaf_order = leaf ^ jnp.arange(leaf_count, dtype=jnp.int32)
    row_map = child_map.reshape(leaf_count, device_rows)[leaf_order].reshape(1, 2 * child_order)
    need = -(-DONE // device_rows)
    spots = leaf_count if small else need
    slots = max(spots, need)
    spot_order = leaf_order if small else jnp.arange(need, dtype=jnp.int32)
    place = jnp.concatenate([jnp.stack([leaf, panel]).astype(jnp.int32), spot_order])

    def root_pieces(value, first=None, second=None):
        if small:
            return over_leaf(value, leaf_count, first, second)
        every = lax.all_gather(value if first is None else after(value, first), "leaf", axis=0)
        return [every[x] for x in range(need)]

    xa, xr, ys, factors = [], [], [], []
    early = 3 if small else 1
    if small:
        root_own = root_pieces(after(high.astype(BF16), pieces[1]))
        picked = [after(picked[0], root_own[-1]), *picked[1:]]
    cols = [over_leaf(picked[step], leaf_count) for step in range(early)]
    if small:
        own_col = over_leaf(picked[STEPS], leaf_count)
        root_all = after(root_all, row_map, place, own_col[-1], cols[0][-1], cols[1][-1])
        roots = [root_pieces(root_all[0])]
    else:
        roots = [root_pieces(root_all[0])]
    done = [roots[0][-1]]
    for step in range(STEPS):
        if step and not small:
            cols.append(over_leaf(after(picked[step], done[-1]), leaf_count))
            roots.append(root_pieces(root_all[step], done[-1]))
        if step == 1 and not small:
            own_part = after(picked[STEPS], done[-1])
            own_col = over_leaf(own_part, leaf_count)
            root_own = root_pieces(high.astype(BF16), own_part)
        root_mine = root_all[step]
        root_step = roots[step]
        step_col = cols[step]
        last = step == STEPS - 1
        args = [*step_col, *root_step, root_mine]
        scratch = [
            pltpu.VMEM((slots, column.shape[0], PANEL), BF16),
            pltpu.VMEM((2, HALF, HALF), F32),
        ]
        if step:
            args += [*own_col, *root_own, *xa, *xr, *ys, mine, rest_block, *factors]
            scratch += [pltpu.VMEM((slots, device_rows, PANEL), BF16)]
        block = jax.ShapeDtypeStruct((device_rows, PANEL), F32)
        if last:
            shapes = [block]
            scratch += [
                pltpu.VMEM((5, HALF, HALF), F32),
                pltpu.VMEM((device_rows, PANEL), F32),
                pltpu.VMEM((device_rows, PANEL), BF16),
                pltpu.VMEM((PANEL, PANEL), BF16),
                pltpu.VMEM((device_rows, PANEL), F32),
                pltpu.VMEM((PANEL, PANEL), F32),
            ]
        else:
            scratch += [pltpu.VMEM(((STEPS - 1 - step) * PANEL, PANEL), F32)]
            shapes = [
                jax.ShapeDtypeStruct(((STEPS - 1 - step) * PANEL, PANEL), BF16),
                block,
                jax.ShapeDtypeStruct((5, HALF, HALF), F32),
            ]
            if step:
                shapes += [
                    jax.ShapeDtypeStruct((device_rows, PANEL), BF16),
                    jax.ShapeDtypeStruct((PANEL, PANEL), BF16),
                    block,
                ]
        out = pl.pallas_call(
            functools.partial(step_kernel, step, leaf_count, spots),
            in_specs=[SMEM_SPEC] + [VMEM_SPEC] * (1 + len(args)),
            out_specs=[VMEM_SPEC] * len(shapes),
            out_shape=shapes,
            scratch_shapes=scratch,
            compiler_params=params,
            cost_estimate=pl.CostEstimate(
                flops=15 * 10**9, transcendentals=0, bytes_accessed=4 * 2**20
            ),
        )(place, row_map, *[near(x) for x in args])
        if last:
            return out[0]
        xa.append(out[0])
        mine = out[1]
        factors.append(out[2])
        rest_block = root_entries
        if step:
            xr.append(out[3])
            ys.append(out[4])
            rest_block = out[5]
        done.append(out[0])
        if small and not last:
            roots.append(root_pieces(root_all[step + 1], done[step], done[step + 1]))
            if step and step + 2 < STEPS:
                cols.append(over_leaf(picked[step + 2], leaf_count, done[step], done[step + 1]))


def solution(mesh):
    spots = (P("leaf", "panel"), P("leaf", "panel"), P(), P())
    return jax.shard_map(
        per_device, mesh=mesh, in_specs=spots, out_specs=P("leaf", "panel"), check_vma=False
    )
```
